32 devices in a mesh: shot: 2 (over y), gy: 4 (over z), gx: 4 (over x, core).
Axes of the slice: x: 2, y: 2, z: 4, core: 2. Of those that a mesh axis runs over, the one named last changes fastest.
Arguments:
- pressure_now: float32 [128, 64, 512], P(('shot', 'gx'), 'gy'), parts along dimension 0, may hold values from -6 to 6
- pressure_old: float32 [128, 64, 512], P(('shot', 'gx'), 'gy'), parts along dimension 0, may hold values from -6 to 6
- classes: int32 [128, 64, 512], P(('shot', 'gx'), 'gy'), parts along dimension 0, may hold values from 0 to 15
- class_table: float32 [16], replicated, may hold values from 0.02 to 0.19
- wavelet: float32 [512], P('shot'), parts along dimension 0, may hold values from -12 to 12
- source_cells: int32 [8], P('shot'), parts along dimension 0, may hold values from 0 to 2097151
- samples: int32 [8], P('shot'), parts along dimension 0, may hold values from 0 to 255
Outputs:
- pressure_next: float32 [128, 64, 512], P(('shot', 'gx'), 'gy'), parts along dimension 0
- pressure_mid: float32 [128, 64, 512], P(('shot', 'gx'), 'gy'), parts along dimension 0
- snapshot_code: float32 [128, 64, 512], P(('shot', 'gx'), 'gy'), parts along dimension 0
The draws below stay inside these ranges and needn't reach their ends.
There are 2 independent parts, one for each index of `shot`. The reference program is written for one: setup_inputs(seed, part) draws one part's arguments, and reference() takes and returns one part's arrays. A program takes and returns all parts, laid end to end along the dimension named above; an argument that names none is the same for every part. Nothing has to cross between parts.
Inputs may be any that keep to these rules, and one draw needn't show every extreme that they name: `source_cells`: decoded as ix * 64 * 512 + iy * 512 + iz.
All inputs are finite; a program needn't handle non-finite values.
Results may differ from the reference program's by a relative error of at most 0.0003.
Values sent between devices are 32-bit elements; how exact they have to be, the bound alone decides.
No kernel may reach another device: no remote copies, remote signals or barrier semaphores. Data moves between devices by JAX's collectives and lax.ppermute only.
A program may use at most 64 MiB of HBM per device.

```python
import math
import jax
import jax.numpy as jnp
from jax import lax

NZ = 512
NCLASS = 16
SHOTS = 4
NT = 256
NX = 64
NY = 64


def with_ends(values, own_key, smallest, high):
    spot = [jax.random.randint(jax.random.fold_in(own_key, axis), (), 0, length) for axis, length in enumerate(values.shape)]
    longest = values.shape.index(max(values.shape))
    beside = spot[:longest] + [(spot[longest] + 1) % values.shape[longest]] + spot[longest + 1:]
    return values.at[tuple(spot)].set(smallest).at[tuple(beside)].set(high)


def level_of(key, dims, split, smallest, top_value):
    factor_of, own = 1.0, jax.random.fold_in(key, 6)
    for axis_at, blocks in split:
        heights = jnp.exp(jax.random.uniform(jax.random.fold_in(own, axis_at), (blocks,), jnp.float32, smallest / len(split), top_value / len(split)))
        factor_of = factor_of * jnp.repeat(heights, dims[axis_at] // blocks).reshape([-1 if axis == axis_at else 1 for axis in range(len(dims))])
    return factor_of


def bell_draw(rng, extent, scale, most, split=(), dtype=jnp.bfloat16):
    drawn = scale * jax.random.normal(rng, extent, jnp.float32)
    if split:
        drawn = drawn * level_of(rng, extent, split, -0.22, 0.18)
    return jnp.clip(drawn, -most, most).astype(dtype)


def setup_inputs(seed: int = 0, part: int = 0) -> dict:
    streams_of = jax.random.split(jax.random.key(seed), 8)
    part_splits = jax.random.split(jax.random.fold_in(streams_of[7], part), 8)
    pressure_now = bell_draw(part_splits[0], (NX, NY, NZ), 1.0, 6.0, ((0, 4), (1, 4)), jnp.float32)
    pressure_old = bell_draw(part_splits[1], (NX, NY, NZ), 1.0, 6.0, ((0, 4), (1, 4)), jnp.float32)
    classes = with_ends(jax.random.randint(part_splits[2], (NX, NY, NZ), 0, NCLASS), jax.random.fold_in(part_splits[2], 1), 0, NCLASS - 1).astype(jnp.int32)
    class_table = jnp.clip(jnp.exp(jax.random.uniform(streams_of[3], (NCLASS,), jnp.float32, math.log(0.02), math.log(0.19))), 0.02, 0.19)
    wavelet = bell_draw(part_splits[4], (NT,), 3.0, 12.0, (), jnp.float32)
    source_cells = with_ends(jax.random.randint(part_splits[5], (SHOTS,), 0, NX * NY * NZ), jax.random.fold_in(part_splits[5], 1), 0, (NX * NY * NZ) - 1).astype(jnp.int32)
    samples = with_ends(jax.random.randint(part_splits[6], (SHOTS,), 0, NT), jax.random.fold_in(part_splits[6], 1), 0, NT - 1).astype(jnp.int32)
    return {"pressure_now": pressure_now, "pressure_old": pressure_old, "classes": classes, "class_table": class_table, "wavelet": wavelet, "source_cells": source_cells, "samples": samples}


STENCIL_WEIGHTS = (-205.0 / 72.0, 8.0 / 5.0, -1.0 / 5.0, 8.0 / 315.0, -1.0 / 560.0)
LIFT_ALPHA = -1.586134342
LIFT_BETA = -0.05298011854
LIFT_GAMMA = 0.8829110762
LIFT_DELTA = 0.4435068522
LIFT_SCALE = 1.149604398
DEAD_ZONE = 0.25
QUANT_STEP = 0.5


def laplace(extended):
    size_x = extended.shape[0] - 8
    size_y = extended.shape[1] - 8
    depth = extended.shape[2]
    depth_padded = jnp.pad(extended[:, 4:4 + size_y, :], ((0, 0), (0, 0), (4, 4)))
    center = extended[4:4 + size_x, 4:4 + size_y, :]
    summed = (3.0 * STENCIL_WEIGHTS[0]) * center
    for offset in range(1, 5):
        beside = extended[4 + offset:4 + offset + size_x, 4:4 + size_y, :] + extended[4 - offset:4 - offset + size_x, 4:4 + size_y, :]
        beside = beside + extended[4:4 + size_x, 4 + offset:4 + offset + size_y, :] + extended[4:4 + size_x, 4 - offset:4 - offset + size_y, :]
        beside = beside + depth_padded[4:4 + size_x, :, 4 + offset:4 + offset + depth] + depth_padded[4:4 + size_x, :, 4 - offset:4 - offset + depth]
        summed = summed + STENCIL_WEIGHTS[offset] * beside
    return summed


def cut_range(field, start, limit, along):
    return lax.slice_in_dim(field, start, limit, 1, along)


def lift_core(padded, along):
    length = padded.shape[along]
    even = lax.slice_in_dim(padded, 0, length, 2, along)
    odd = lax.slice_in_dim(padded, 1, length, 2, along)
    half = even.shape[along]
    odd_one = cut_range(odd, 0, half - 1, along) + LIFT_ALPHA * (cut_range(even, 0, half - 1, along) + cut_range(even, 1, half, along))
    even_one = cut_range(even, 1, half - 1, along) + LIFT_BETA * (cut_range(odd_one, 0, half - 2, along) + cut_range(odd_one, 1, half - 1, along))
    odd_two = cut_range(odd_one, 1, half - 2, along) + LIFT_GAMMA * (cut_range(even_one, 0, half - 3, along) + cut_range(even_one, 1, half - 2, along))
    even_two = cut_range(even_one, 1, half - 3, along) + LIFT_DELTA * (cut_range(odd_two, 0, half - 4, along) + cut_range(odd_two, 1, half - 3, along))
    low_band = even_two / LIFT_SCALE
    high_band = cut_range(odd_two, 1, half - 3, along) * LIFT_SCALE
    joined = jnp.stack([low_band, high_band], along + 1)
    shape = low_band.shape[:along] + (2 * low_band.shape[along],) + low_band.shape[along + 1:]
    return joined.reshape(shape)


def reflect_lift(field, along):
    widths = [(0, 0)] * field.ndim
    widths[along] = (4, 4)
    return lift_core(jnp.pad(field, widths, mode="reflect"), along)


def quantize(values):
    return jnp.sign(values) * jnp.maximum(jnp.abs(values) - DEAD_ZONE, 0.0) / QUANT_STEP


def source_field(source_cells, samples, wavelet, step_index):
    cell_x = source_cells // (NY * NZ)
    cell_y = (source_cells // NZ) % NY
    cell_z = source_cells % NZ
    amplitude = wavelet[(samples + step_index) % NT]
    return jnp.zeros((NX, NY, NZ), jnp.float32).at[cell_x, cell_y, cell_z].add(amplitude)


def advance(field, older, courant, source):
    extended = jnp.pad(field, ((4, 4), (4, 4), (0, 0)))
    return 2.0 * field - older + courant * laplace(extended) + source


def reference(pressure_now, pressure_old, classes, class_table, wavelet, source_cells, samples):
    courant = class_table[classes]
    pressure_mid = advance(pressure_now, pressure_old, courant, source_field(source_cells, samples, wavelet, 0))
    pressure_next = advance(pressure_mid, pressure_now, courant, source_field(source_cells, samples, wavelet, 1))
    lifted = reflect_lift(pressure_next, 2)
    lifted = reflect_lift(lifted, 0)
    lifted = reflect_lift(lifted, 1)
    return pressure_next, pressure_mid, quantize(lifted)
```

```python
import functools

import jax
import jax.numpy as jnp
from jax import lax
from jax.experimental import pallas as pl
from jax.experimental.pallas import tpu as pltpu
from jax.sharding import PartitionSpec as P

STENCIL_WEIGHTS = (-205.0 / 72.0, 8.0 / 5.0, -1.0 / 5.0, 8.0 / 315.0, -1.0 / 560.0)
LIFT_ALPHA = -1.586134342
LIFT_BETA = -0.05298011854
LIFT_GAMMA = 0.8829110762
LIFT_DELTA = 0.4435068522
LIFT_SCALE = 1.149604398
DEAD_ZONE = 0.25
QUANT_STEP = 0.5

HALO = 4
LANES = 128
SUB = 8


def iota(axis):
    return lax.broadcasted_iota(jnp.int32, (SUB, LANES), axis)


def rolled(value, shift, axis):
    size = value.shape[axis]
    shift = shift % size
    return value if shift == 0 else pltpu.roll(value, shift, axis)


def parity(axis):
    index = lax.axis_index(axis)
    return lax.rem(index, 2) == 0, index == 0, index == lax.axis_size(axis) - 1


def pack_x(field, low, high, even, x_first, x_second):
    for slot, (down, up) in enumerate(zip(low, high)):
        for tile in range(x_first.shape[1]):
            for y_tile in range(x_first.shape[2] // SUB):
                below, above = field(down, tile, y_tile), field(up, tile, y_tile)
                where = (slot, tile, pl.ds(y_tile * SUB, SUB))
                x_first[where] = jnp.where(even, above, below)
                x_second[where] = jnp.where(even, below, above)


def pack_y(field, rows_x, tiles, y_tiles, even, y_first, y_second):
    lower = iota(0) < HALO

    def step(x, _):
        for pair in range(tiles // 2):
            picked = []
            for tile in (2 * pair, 2 * pair + 1):
                below = field(x, tile, 0)
                above = rolled(field(x, tile, y_tiles - 1), HALO, 0)
                picked.append((jnp.where(even, above, below), jnp.where(even, below, above)))
            y_first[x, pair] = jnp.where(lower, picked[0][0], rolled(picked[1][0], HALO, 0))
            y_second[x, pair] = jnp.where(lower, picked[0][1], rolled(picked[1][1], HALO, 0))
        return 0

    lax.fori_loop(0, rows_x, step, 0)


def zero_pads(padded, rows_x, rows_y):
    zero = jnp.zeros((SUB, LANES), jnp.float32)
    tiles = padded.shape[1]
    for x in list(range(HALO)) + list(range(rows_x + HALO, rows_x + 2 * HALO)):
        for tile in range(tiles):
            for y in range(SUB, rows_y + SUB, SUB):
                padded[x, tile, pl.ds(y, SUB)] = zero

    def step(x, _):
        for tile in range(tiles):
            padded[x + HALO, tile, pl.ds(0, SUB)] = zero
            padded[x + HALO, tile, pl.ds(rows_y + SUB, SUB)] = zero
        return 0

    lax.fori_loop(0, rows_x, step, 0)


def padded_vector(padded):
    return lambda x, tile, y_tile: padded[x + HALO, tile, pl.ds(SUB + y_tile * SUB, SUB)]


def sends_kernel(now, padded, x_first, x_second, y_first, y_second, sems):
    rows_x, rows_y, depth = now.shape
    tiles = depth // LANES
    copies = [
        pltpu.make_async_copy(
            now.at[:, :, pl.ds(tile * LANES, LANES)],
            padded.at[pl.ds(HALO, rows_x), tile, pl.ds(SUB, rows_y), :],
            sems.at[tile],
        )
        for tile in range(tiles)
    ]
    for copy in copies:
        copy.start()
    zero_pads(padded, rows_x, rows_y)
    even_x, _, _ = parity("gx")
    even_y, _, _ = parity("gy")
    for copy in copies:
        copy.wait()
    field = padded_vector(padded)
    pack_x(
        field, range(HALO), range(rows_x - HALO, rows_x), even_x, x_first, x_second
    )
    pack_y(field, rows_x, tiles, rows_y // SUB, even_y, y_first, y_second)


def local_laplace(padded, x, tiles, y_tile):
    lane = iota(1)
    row, y = x + HALO, SUB + y_tile * SUB
    center = [padded[row, tile, pl.ds(y, SUB)] for tile in range(tiles)]
    zero = jnp.zeros((SUB, LANES), jnp.float32)
    total = [3.0 * STENCIL_WEIGHTS[0] * value for value in center]
    for offset in range(1, HALO + 1):
        up = [rolled(value, -offset, 1) for value in center] + [zero]
        down = [zero] + [rolled(value, offset, 1) for value in center]
        for tile in range(tiles):
            beside = jnp.where(lane < LANES - offset, up[tile], up[tile + 1])
            beside = beside + jnp.where(lane >= offset, down[tile + 1], down[tile])
            beside = beside + (
                padded[row + offset, tile, pl.ds(y, SUB)]
                + padded[row - offset, tile, pl.ds(y, SUB)]
            )
            beside = beside + (
                padded[row, tile, pl.ds(y + offset, SUB)]
                + padded[row, tile, pl.ds(y - offset, SUB)]
            )
            total[tile] = total[tile] + STENCIL_WEIGHTS[offset] * beside
    return center, total


def add_sources(base, cells, samples, wavelet, step_index, rows_x, rows_y, depth):
    all_y = rows_y * lax.axis_size("gy")
    start_x = lax.axis_index("gx") * rows_x
    start_y = lax.axis_index("gy") * rows_y
    lane = lax.broadcasted_iota(jnp.int32, (1, LANES), 1)
    for shot in range(cells.shape[0]):
        cell = cells[shot]
        x = lax.div(cell, all_y * depth) - start_x
        y = lax.rem(lax.div(cell, depth), all_y) - start_y
        z = lax.rem(cell, depth)
        inside = (x >= 0) & (x < rows_x) & (y >= 0) & (y < rows_y)

        @pl.when(inside)
        def _():
            value = wavelet[lax.rem(samples[shot] + step_index, wavelet.shape[0])]
            where = (x, lax.div(z, LANES), pl.ds(y, 1))
            base[where] = base[where] + jnp.where(lane == lax.rem(z, LANES), value, 0.0)


def first_local_kernel(
    padded, old, classes, table, wavelet, cells, samples, base, courant, blank
):
    rows_x, rows_y, depth = old.shape
    tiles = depth // LANES
    lane = iota(1)
    entries = jnp.zeros((SUB, LANES), jnp.float32)
    for material in range(table.shape[0]):
        entries = jnp.where(lane == material, table[material], entries)

    def step(x, _):
        for y_tile in range(rows_y // SUB):
            center, total = local_laplace(padded, x, tiles, y_tile)
            y = pl.ds(y_tile * SUB, SUB)
            for tile in range(tiles):
                z = pl.ds(tile * LANES, LANES)
                speed = jnp.take_along_axis(entries, classes[x, y, z], axis=1)
                courant[x, tile, y] = speed
                base[x, tile, y] = 2.0 * center[tile] - old[x, y, z] + speed * total[tile]
        return 0

    lax.fori_loop(0, rows_x, step, 0)
    add_sources(base, cells, samples, wavelet, 0, rows_x, rows_y, depth)
    zero_pads(blank, rows_x, rows_y)


def second_local_kernel(
    padded, before, courant, wavelet, cells, samples, base, mid, sems
):
    rows_x, rows_y, depth = mid.shape
    tiles = depth // LANES
    copies = [
        pltpu.make_async_copy(
            padded.at[pl.ds(HALO, rows_x), tile, pl.ds(SUB, rows_y), :],
            mid.at[:, :, pl.ds(tile * LANES, LANES)],
            sems.at[tile],
        )
        for tile in range(tiles)
    ]
    for copy in copies:
        copy.start()

    def step(x, _):
        for y_tile in range(rows_y // SUB):
            center, total = local_laplace(padded, x, tiles, y_tile)
            y = pl.ds(y_tile * SUB, SUB)
            for tile in range(tiles):
                earlier = before[x + HALO, tile, pl.ds(SUB + y_tile * SUB, SUB)]
                base[x, tile, y] = (
                    2.0 * center[tile] - earlier + courant[x, tile, y] * total[tile]
                )
        return 0

    lax.fori_loop(0, rows_x, step, 0)
    add_sources(base, cells, samples, wavelet, 1, rows_x, rows_y, depth)
    for copy in copies:
        copy.wait()


def sides(first, second, even, at_first, at_last):
    low = jnp.where(even, second, first)
    high = jnp.where(even, first, second)
    return jnp.where(at_first, 0.0, low), jnp.where(at_last, 0.0, high)


def add_halos(base, courant, x_first, x_second, y_first, y_second, x_halo, y_halo, store):
    rows_x, tiles, rows_y, _ = base.shape
    y_tiles = rows_y // SUB
    even_x, first_x, last_x = parity("gx")
    even_y, first_y, last_y = parity("gy")
    lower = iota(0) < HALO
    zero = jnp.zeros((SUB, LANES), jnp.float32)
    for slot in range(HALO):
        for tile in range(tiles):
            for y_tile in range(y_tiles):
                y = pl.ds(y_tile * SUB, SUB)
                low, high = sides(
                    x_first[slot, tile, y], x_second[slot, tile, y], even_x, first_x, last_x
                )
                x_halo[slot, tile, y] = low
                x_halo[HALO + slot, tile, y] = high

    def spread(x, _):
        for pair in range(tiles // 2):
            low, high = sides(y_first[x, pair], y_second[x, pair], even_y, first_y, last_y)
            for half, tile in enumerate((2 * pair, 2 * pair + 1)):
                y_halo[x, tile, pl.ds(0, SUB)] = jnp.where(lower, rolled(low, half * HALO, 0), 0.0)
                y_halo[x, tile, pl.ds(SUB, SUB)] = zero
                y_halo[x, tile, pl.ds(2 * SUB, SUB)] = jnp.where(
                    lower, rolled(high, half * HALO, 0), 0.0
                )
        return 0

    lax.fori_loop(0, rows_x, spread, 0)

    def finish(x, x_terms):
        for y_tile in range(y_tiles):
            y = pl.ds(y_tile * SUB, SUB)
            done = []
            for tile in range(tiles):
                beyond = None
                terms = [(w, x_halo[slot, tile, y]) for w, slot in x_terms]
                for offset in range(1, HALO + 1):
                    weight = STENCIL_WEIGHTS[offset]
                    if y_tile == 0:
                        terms.append((weight, y_halo[x, tile, pl.ds(HALO - offset, SUB)]))
                    if y_tile == y_tiles - 1:
                        terms.append((weight, y_halo[x, tile, pl.ds(SUB + offset, SUB)]))
                for weight, value in terms:
                    beyond = weight * value if beyond is None else beyond + weight * value
                value = base[x, tile, y]
                if beyond is not None:
                    value = value + courant[x, tile, y] * beyond
                done.append(value)
            store(x, y_tile, done)

    for x in list(range(HALO)) + list(range(rows_x - HALO, rows_x)):
        x_terms = []
        for offset in range(1, HALO + 1):
            if x - offset < 0:
                x_terms.append((STENCIL_WEIGHTS[offset], HALO + x - offset))
            if x + offset >= rows_x:
                x_terms.append((STENCIL_WEIGHTS[offset], HALO + x + offset - rows_x))
        finish(x, x_terms)

    def inner(x, _):
        finish(x, ())
        return 0

    lax.fori_loop(HALO, rows_x - HALO, inner, 0)


def mid_kernel(
    base, courant, x_in, x_in_2, y_in, y_in_2, blank,
    padded, x_first, x_second, y_first, y_second, x_halo, y_halo,
):
    rows_x, tiles, rows_y, _ = base.shape
    even_x, _, _ = parity("gx")
    even_y, _, _ = parity("gy")

    def store(x, y_tile, values):
        for tile, value in enumerate(values):
            padded[x + HALO, tile, pl.ds(SUB + y_tile * SUB, SUB)] = value

    add_halos(base, courant, x_in, x_in_2, y_in, y_in_2, x_halo, y_halo, store)
    field = padded_vector(padded)
    pack_x(field, range(HALO), range(rows_x - HALO, rows_x), even_x, x_first, x_second)
    pack_y(field, rows_x, tiles, rows_y // SUB, even_y, y_first, y_second)


def lift_depth(values):
    lane = iota(1)
    odd = lax.rem(lane, 2) == 1
    tiles = len(values)
    for weight, on_odd in (
        (LIFT_ALPHA, True), (LIFT_BETA, False), (LIFT_GAMMA, True), (LIFT_DELTA, False)
    ):
        factor = jnp.where(odd if on_odd else ~odd, weight, 0.0)
        up = [rolled(value, -1, 1) for value in values]
        down = [rolled(value, 1, 1) for value in values]
        result = []
        for tile in range(tiles):
            above = up[tile + 1] if tile + 1 < tiles else down[tile]
            below = down[tile - 1] if tile else up[tile]
            beside = jnp.where(lane < LANES - 1, up[tile], above)
            beside = beside + jnp.where(lane >= 1, down[tile], below)
            result.append(values[tile] + factor * beside)
        values = result
    return values


def next_kernel(
    base, courant, x_in, x_in_2, y_in, y_in_2,
    field, lifted, x_first, x_second, x_halo, y_halo,
):
    rows_x, tiles, rows_y, _ = base.shape
    even_x, _, _ = parity("gx")

    def store(x, y_tile, values):
        y = pl.ds(y_tile * SUB, SUB)
        for tile, value in enumerate(values):
            field[x, tile, y] = value
        for tile, value in enumerate(lift_depth(values)):
            lifted[x, tile, y] = value

    add_halos(base, courant, x_in, x_in_2, y_in, y_in_2, x_halo, y_halo, store)
    for tile in range(tiles):
        for y_tile in range(rows_y // SUB):
            y = pl.ds(y_tile * SUB, SUB)
            start = [lifted[x, tile, y] for x in range(3)]
            end = [lifted[x, tile, y] for x in range(rows_x - 4, rows_x)]
            low = (start[0], start[1] + LIFT_ALPHA * (start[0] + start[2]))
            high = (
                end[2] + LIFT_BETA * (end[1] + LIFT_ALPHA * (end[0] + end[2])),
                end[3] + LIFT_ALPHA * end[2],
            )
            for slot in range(2):
                x_first[slot, tile, y] = jnp.where(even_x, high[slot], low[slot])
                x_second[slot, tile, y] = jnp.where(even_x, low[slot], high[slot])


def write_kernel(field, out, sems):
    tiles = field.shape[1]
    copies = [
        pltpu.make_async_copy(
            field.at[:, tile], out.at[:, :, pl.ds(tile * LANES, LANES)], sems.at[tile]
        )
        for tile in range(tiles)
    ]
    for copy in copies:
        copy.start()
    for copy in copies:
        copy.wait()


def lift_x_kernel(lifted, x_in, x_in_2, out, y_first, y_second):
    rows_x, tiles, rows_y, _ = lifted.shape
    y_tiles = rows_y // SUB
    half = rows_x // 2
    even_x, first_x, last_x = parity("gx")
    even_y, _, _ = parity("gy")

    def column(tile, _):
        for y_tile in range(y_tiles):
            y = pl.ds(y_tile * SUB, SUB)
            got = [
                (
                    jnp.where(even_x, x_in_2[slot, tile, y], x_in[slot, tile, y]),
                    jnp.where(even_x, x_in[slot, tile, y], x_in_2[slot, tile, y]),
                )
                for slot in range(2)
            ]
            even = [lifted[2 * i, tile, y] for i in range(half)]
            odd = [lifted[2 * i + 1, tile, y] for i in range(half)]
            beyond = jnp.where(last_x, even[-1], got[0][1])
            even.append(beyond)
            odd = [odd[i] + LIFT_ALPHA * (even[i] + even[i + 1]) for i in range(half)]
            before = got[1][0] + LIFT_ALPHA * even[0]
            odd = [jnp.where(first_x, odd[0], before)] + odd
            last = even.pop() + LIFT_BETA * (odd[-1] + got[1][1])
            even = [even[i] + LIFT_BETA * (odd[i] + odd[i + 1]) for i in range(half)]
            even.append(jnp.where(last_x, even[-1], last))
            start = got[0][0] + LIFT_BETA * odd[0]
            start = odd[0] + LIFT_GAMMA * (start + even[0])
            odd = [odd[i + 1] + LIFT_GAMMA * (even[i] + even[i + 1]) for i in range(half)]
            padded = [jnp.where(first_x, odd[0], start)] + odd
            even = [even[i] + LIFT_DELTA * (padded[i] + padded[i + 1]) for i in range(half)]
            for i in range(half):
                out[2 * i, tile, y] = even[i]
                out[2 * i + 1, tile, y] = odd[i]
        return 0

    lax.fori_loop(0, tiles, column, 0)
    sub = iota(0)
    per = SUB // 2

    def pack(x, _):
        for group in range(tiles // per):
            packed = [None, None]
            for place in range(per):
                tile = group * per + place
                start = out[x, tile, pl.ds(0, SUB)]
                end = out[x, tile, pl.ds((y_tiles - 1) * SUB, SUB)]
                beside = rolled(start, 1, 0) + rolled(start, -1, 0)
                low = jnp.where(sub == 0, start, start + LIFT_ALPHA * beside)
                below = rolled(end, 1, 0)
                odd = end + LIFT_ALPHA * (below + rolled(end, -1, 0))
                high = jnp.where(
                    sub == SUB - 1,
                    end + LIFT_ALPHA * below,
                    end + LIFT_BETA * rolled(odd, 1, 0),
                )
                high = rolled(high, 2, 0)
                picked = (jnp.where(even_y, high, low), jnp.where(even_y, low, high))
                for side in range(2):
                    value = rolled(picked[side], 2 * place, 0)
                    if place:
                        value = jnp.where(sub >= 2 * place, value, packed[side])
                    packed[side] = value
            y_first[x, group] = packed[0]
            y_second[x, group] = packed[1]
        return 0

    lax.fori_loop(0, rows_x, pack, 0)


def lift_y_kernel(lifted, y_in, y_in_2, out, codes, sems):
    rows_x, tiles, rows_y, _ = lifted.shape
    even_y, first_y, last_y = parity("gy")
    sub = iota(0)
    z_odd = lax.rem(iota(1), 2) == 1
    per = SUB // 2
    top = sub == SUB - 1
    bottom = sub == 0
    at_first = bottom & first_y
    at_last = top & last_y

    def scale(x_odd, y_odd):
        power = (1 if x_odd else -1) + (1 if y_odd else -1)
        return jnp.where(z_odd, LIFT_SCALE ** (power + 1), LIFT_SCALE ** (power - 1))

    def code(value):
        kept = jnp.maximum(value - DEAD_ZONE, 0.0) + jnp.minimum(value + DEAD_ZONE, 0.0)
        return kept * (1.0 / QUANT_STEP)

    def row(x, x_odd):
        for group in range(tiles // per):
            low = jnp.where(even_y, y_in_2[x, group], y_in[x, group])
            high = jnp.where(even_y, y_in[x, group], y_in_2[x, group])
            for place in range(per):
                tile = group * per + place
                even = lifted[x, tile, pl.ds(0, SUB, stride=2)]
                odd = lifted[x, tile, pl.ds(1, SUB, stride=2)]
                far = rolled(high, SUB - 1 - 2 * place, 0)
                far_odd = rolled(high, SUB - 2 - 2 * place, 0)
                near = rolled(low, -2 * place, 0)
                near_odd = rolled(low, -2 * place - 1, 0)
                beyond = jnp.where(at_last, even, jnp.where(top, far, rolled(even, -1, 0)))
                odd = odd + LIFT_ALPHA * (even + beyond)
                before = near_odd + LIFT_ALPHA * even
                under = jnp.where(at_first, odd, jnp.where(bottom, before, rolled(odd, 1, 0)))
                last = far + LIFT_BETA * (odd + far_odd)
                even = even + LIFT_BETA * (odd + under)
                beyond = jnp.where(at_last, even, jnp.where(top, last, rolled(even, -1, 0)))
                start = before + LIFT_GAMMA * (near + LIFT_BETA * before + even)
                odd = odd + LIFT_GAMMA * (even + beyond)
                under = jnp.where(at_first, odd, jnp.where(bottom, start, rolled(odd, 1, 0)))
                even = even + LIFT_DELTA * (odd + under)
                codes[x, tile, pl.ds(0, SUB, stride=2)] = code(even * scale(x_odd, False))
                codes[x, tile, pl.ds(1, SUB, stride=2)] = code(odd * scale(x_odd, True))

    def step(pair, _):
        row(2 * pair, False)
        row(2 * pair + 1, True)
        return 0

    lax.fori_loop(0, rows_x // 2, step, 0)
    write_kernel(codes, out, sems)


def whole(count):
    return [pl.BlockSpec(memory_space=pltpu.VMEM)] * count


def scalars(count):
    return [pl.BlockSpec(memory_space=pltpu.SMEM)] * count


def far(count):
    return [pl.BlockSpec(memory_space=pltpu.HBM)] * count


def call(kernel, in_specs, out_specs, out_shape, scratch=(), cost=1.0, aliases=None, **kwargs):
    return pl.pallas_call(
        kernel,
        in_specs=in_specs,
        out_specs=out_specs,
        out_shape=[jax.ShapeDtypeStruct(shape, jnp.float32) for shape in out_shape],
        scratch_shapes=list(scratch),
        input_output_aliases=aliases or {},
        compiler_params=pltpu.CompilerParams(vmem_limit_bytes=16 << 20),
        cost_estimate=pl.CostEstimate(
            flops=int(cost * 1e6), bytes_accessed=int(cost * 1e6), transcendentals=0
        ),
        **kwargs,
    )


def swaps(names, counts, partner):
    pairs = []
    for y in range(counts[0]):
        for x in range(counts[1]):
            target = partner(y, x)
            pairs.append((y * counts[1] + x, target[0] * counts[1] + target[1]))
    return functools.partial(lax.ppermute, axis_name=names, perm=pairs)


def exchanges(count_y, count_x):
    names = ("gy", "gx")
    counts = (count_y, count_x)

    def second(index, count):
        return (index + 1) % count if index % 2 else (index - 1) % count

    x_first = swaps(names, counts, lambda y, x: (y, x ^ 1))
    x_second = swaps(names, counts, lambda y, x: (y, second(x, count_x)))
    y_first = swaps(names, counts, lambda y, x: (y ^ 1, x))

    def inner_y(y, x):
        return (second(y, count_y), x) if 0 < y < count_y - 1 else (y, x ^ 1)

    return x_first, x_second, y_first, swaps(names, counts, inner_y)


def shards(pressure_now, pressure_old, classes, class_table, wavelet, source_cells, samples):
    rows_x, rows_y, depth = pressure_now.shape
    tiles = depth // LANES
    swap_x, swap_x_2, swap_y, swap_y_2 = exchanges(lax.axis_size("gy"), lax.axis_size("gx"))
    padded_shape = (rows_x + 2 * HALO, tiles, rows_y + 2 * SUB, LANES)
    block_shape = (rows_x, tiles, rows_y, LANES)
    x_shape = (HALO, tiles, rows_y, LANES)
    y_shape = (rows_x, tiles // 2, SUB, LANES)
    x_lift_shape = (2, tiles, rows_y, LANES)
    y_lift_shape = (rows_x, tiles // 4, SUB, LANES)
    natural = (rows_x, rows_y, depth)
    sems = pltpu.SemaphoreType.DMA((tiles,))
    halos = (
        pltpu.VMEM((2 * HALO, tiles, rows_y, LANES), jnp.float32),
        pltpu.VMEM((rows_x, tiles, 3 * SUB, LANES), jnp.float32),
    )

    def star(sends):
        x_1, x_2, y_1, y_2 = sends
        got_y, got_y_2 = swap_y(y_1), swap_y_2(y_2)
        got_x_2, got_x = swap_x_2(x_2), swap_x(x_1)
        return got_x, got_x_2, got_y, got_y_2

    now, *sends = call(
        sends_kernel, far(1), whole(5), [padded_shape, x_shape, x_shape, y_shape, y_shape],
        (sems,), name="sends",
    )(pressure_now)
    got = star(sends)
    base, courant, blank = call(
        first_local_kernel, whole(3) + scalars(4), whole(3),
        [block_shape, block_shape, padded_shape], cost=4.0, name="first_local",
    )(now, pressure_old, classes, class_table, wavelet, source_cells, samples)
    mid, *sends = call(
        mid_kernel, whole(7), whole(5), [padded_shape, x_shape, x_shape, y_shape, y_shape],
        halos, aliases={6: 0}, name="mid",
    )(base, courant, *got, blank)
    got = star(sends)
    base, pressure_mid = call(
        second_local_kernel, whole(3) + scalars(3), whole(1) + far(1), [block_shape, natural],
        (sems,), cost=4.0, name="second_local",
    )(mid, now, courant, wavelet, source_cells, samples)
    field, lifted, *sends = call(
        next_kernel, whole(6), whole(4), [block_shape, block_shape, x_lift_shape, x_lift_shape],
        halos, name="next",
    )(base, courant, *got)
    got_2, got = swap_x_2(sends[1]), swap_x(sends[0])
    (pressure_next,) = call(write_kernel, whole(1), far(1), [natural], (sems,), name="write")(field)
    lifted, *sends = call(
        lift_x_kernel, whole(3), whole(3), [block_shape, y_lift_shape, y_lift_shape], name="lift_x"
    )(lifted, got, got_2)
    got, got_2 = swap_y(sends[0]), swap_y_2(sends[1])
    (snapshot_code,) = call(
        lift_y_kernel, whole(3), far(1), [natural],
        (pltpu.VMEM(block_shape, jnp.float32), sems), name="lift_y",
    )(lifted, got, got_2)
    return (pressure_next, pressure_mid, snapshot_code)


def solution(mesh):
    block = P(("shot", "gx"), "gy", None)
    return jax.shard_map(
        shards,
        mesh=mesh,
        in_specs=(block, block, block, P(), P("shot"), P("shot"), P("shot")),
        out_specs=(block, block, block),
        check_vma=False,
    )
```

```python
import functools

import jax
import jax.numpy as jnp
from jax import lax
from jax.experimental import pallas as pl
from jax.experimental.pallas import tpu as pltpu
from jax.sharding import PartitionSpec as P

STENCIL_WEIGHTS = (-205.0 / 72.0, 8.0 / 5.0, -1.0 / 5.0, 8.0 / 315.0, -1.0 / 560.0)
LIFT_ALPHA = -1.586134342
LIFT_BETA = -0.05298011854
LIFT_GAMMA = 0.8829110762
LIFT_DELTA = 0.4435068522
LIFT_SCALE = 1.149604398
DEAD_ZONE = 0.25
QUANT_STEP = 0.5

HALO = 4
LANES = 128
SUB = 8


def iota(axis):
    return lax.broadcasted_iota(jnp.int32, (SUB, LANES), axis)


def rolled(value, shift, axis):
    size = value.shape[axis]
    shift = shift % size
    return value if shift == 0 else pltpu.roll(value, shift, axis)


def parity(axis):
    index = lax.axis_index(axis)
    return lax.rem(index, 2) == 0, index == 0, index == lax.axis_size(axis) - 1


def pack_x(field, low, high, even, x_first, x_second):
    for slot, (down, up) in enumerate(zip(low, high)):
        for tile in range(x_first.shape[1]):
            for y_tile in range(x_first.shape[2] // SUB):
                below, above = field(down, tile, y_tile), field(up, tile, y_tile)
                where = (slot, tile, pl.ds(y_tile * SUB, SUB))
                x_first[where] = jnp.where(even, above, below)
                x_second[where] = jnp.where(even, below, above)


def pack_y(field, rows_x, tiles, y_tiles, even, y_first, y_second):
    lower = iota(0) < HALO

    def step(x, _):
        for pair in range(tiles // 2):
            picked = []
            for tile in (2 * pair, 2 * pair + 1):
                below = field(x, tile, 0)
                above = rolled(field(x, tile, y_tiles - 1), HALO, 0)
                picked.append((jnp.where(even, above, below), jnp.where(even, below, above)))
            y_first[x, pair] = jnp.where(lower, picked[0][0], rolled(picked[1][0], HALO, 0))
            y_second[x, pair] = jnp.where(lower, picked[0][1], rolled(picked[1][1], HALO, 0))
        return 0

    lax.fori_loop(0, rows_x, step, 0, unroll=4)


def zero_pads(padded, rows_x, rows_y):
    zero = jnp.zeros((SUB, LANES), jnp.float32)
    tiles = padded.shape[1]
    for x in list(range(HALO)) + list(range(rows_x + HALO, rows_x + 2 * HALO)):
        for tile in range(tiles):
            for y in range(SUB, rows_y + SUB, SUB):
                padded[x, tile, pl.ds(y, SUB)] = zero

    def step(x, _):
        for tile in range(tiles):
            padded[x + HALO, tile, pl.ds(0, SUB)] = zero
            padded[x + HALO, tile, pl.ds(rows_y + SUB, SUB)] = zero
        return 0

    lax.fori_loop(0, rows_x, step, 0)


def padded_vector(padded):
    return lambda x, tile, y_tile: padded[x + HALO, tile, pl.ds(SUB + y_tile * SUB, SUB)]


def sends_kernel(now, x_first, x_second, y_first, y_second):
    rows_x, rows_y, depth = now.shape
    even_x, _, _ = parity("gx")
    even_y, _, _ = parity("gy")

    def field(x, tile, y_tile):
        return now[x, pl.ds(y_tile * SUB, SUB), pl.ds(tile * LANES, LANES)]

    pack_x(field, range(HALO), range(rows_x - HALO, rows_x), even_x, x_first, x_second)
    pack_y(field, rows_x, depth // LANES, rows_y // SUB, even_y, y_first, y_second)


def local_laplace(padded, x, tiles, y_tile):
    lane = iota(1)
    row, y = x + HALO, SUB + y_tile * SUB
    center = [padded[row, tile, pl.ds(y, SUB)] for tile in range(tiles)]
    zero = jnp.zeros((SUB, LANES), jnp.float32)
    total = [3.0 * STENCIL_WEIGHTS[0] * value for value in center]
    for offset in range(1, HALO + 1):
        up = [rolled(value, -offset, 1) for value in center] + [zero]
        down = [zero] + [rolled(value, offset, 1) for value in center]
        for tile in range(tiles):
            beside = jnp.where(lane < LANES - offset, up[tile], up[tile + 1])
            beside = beside + jnp.where(lane >= offset, down[tile + 1], down[tile])
            beside = beside + (
                padded[row + offset, tile, pl.ds(y, SUB)]
                + padded[row - offset, tile, pl.ds(y, SUB)]
            )
            beside = beside + (
                padded[row, tile, pl.ds(y + offset, SUB)]
                + padded[row, tile, pl.ds(y - offset, SUB)]
            )
            total[tile] = total[tile] + STENCIL_WEIGHTS[offset] * beside
    return center, total


def add_sources(base, cells, samples, wavelet, step_index, rows_x, rows_y, depth):
    all_y = rows_y * lax.axis_size("gy")
    start_x = lax.axis_index("gx") * rows_x
    start_y = lax.axis_index("gy") * rows_y
    lane = lax.broadcasted_iota(jnp.int32, (1, LANES), 1)
    for shot in range(cells.shape[0]):
        cell = cells[shot]
        x = lax.div(cell, all_y * depth) - start_x
        y = lax.rem(lax.div(cell, depth), all_y) - start_y
        z = lax.rem(cell, depth)
        inside = (x >= 0) & (x < rows_x) & (y >= 0) & (y < rows_y)

        @pl.when(inside)
        def _():
            value = wavelet[lax.rem(samples[shot] + step_index, wavelet.shape[0])]
            where = (x, lax.div(z, LANES), pl.ds(y, 1))
            base[where] = base[where] + jnp.where(lane == lax.rem(z, LANES), value, 0.0)


def start_all(copies):
    for copy in copies:
        copy.start()
    return copies


def wait_all(copies):
    for copy in copies:
        copy.wait()


def paired(sources, targets, sems):
    return [
        pltpu.make_async_copy(source, target, sems.at[place])
        for place, (source, target) in enumerate(zip(sources, targets))
    ]


def first_local_kernel(
    now, old, classes, table, wavelet, cells, samples,
    padded, base, courant, blank,
    old_here, classes_here, table_here, wavelet_here, cells_here, samples_here, sems,
):
    rows_x, rows_y, depth = old.shape
    tiles = depth // LANES
    lane = iota(1)
    copies = start_all(
        paired(
            (table, classes, old, wavelet, cells, samples),
            (table_here, classes_here, old_here, wavelet_here, cells_here, samples_here),
            sems,
        )
    )
    zero_pads(padded, rows_x, rows_y)

    def spread(x, _):
        for tile in range(tiles):
            for y in range(0, rows_y, SUB):
                padded[x + HALO, tile, pl.ds(SUB + y, SUB)] = now[
                    x, pl.ds(y, SUB), pl.ds(tile * LANES, LANES)
                ]
        return 0

    lax.fori_loop(0, rows_x, spread, 0, unroll=4)

    def sums(x, _):
        for y_tile in range(rows_y // SUB):
            _, total = local_laplace(padded, x, tiles, y_tile)
            for tile in range(tiles):
                base[x, tile, pl.ds(y_tile * SUB, SUB)] = total[tile]
        return 0

    lax.fori_loop(0, rows_x, sums, 0, unroll=4)
    wait_all(copies)
    entries = jnp.zeros((SUB, LANES), jnp.float32)
    for material in range(table.shape[0]):
        entries = jnp.where(lane == material, table_here[material], entries)

    def step(x, _):
        for y_tile in range(rows_y // SUB):
            y = pl.ds(y_tile * SUB, SUB)
            for tile in range(tiles):
                z = pl.ds(tile * LANES, LANES)
                speed = jnp.take_along_axis(entries, classes_here[x, y, z], axis=1)
                courant[x, tile, y] = speed
                base[x, tile, y] = (
                    2.0 * now[x, y, z] - old_here[x, y, z] + speed * base[x, tile, y]
                )
        return 0

    lax.fori_loop(0, rows_x, step, 0, unroll=4)
    add_sources(
        base, cells_here, samples_here, wavelet_here, 0, rows_x, rows_y, depth
    )
    zero_pads(blank, rows_x, rows_y)


def second_local_kernel(
    padded, before, courant, wavelet, cells, samples,
    base, mid,
    wavelet_here, cells_here, samples_here, sems,
):
    rows_x, rows_y, depth = mid.shape
    tiles = depth // LANES
    copies = start_all(
        paired(
            [wavelet, cells, samples]
            + [padded.at[pl.ds(HALO, rows_x), t, pl.ds(SUB, rows_y), :] for t in range(tiles)],
            [wavelet_here, cells_here, samples_here]
            + [mid.at[:, :, pl.ds(t * LANES, LANES)] for t in range(tiles)],
            sems,
        )
    )

    def step(x, _):
        for y_tile in range(rows_y // SUB):
            center, total = local_laplace(padded, x, tiles, y_tile)
            y = pl.ds(y_tile * SUB, SUB)
            for tile in range(tiles):
                earlier = before[x + HALO, tile, pl.ds(SUB + y_tile * SUB, SUB)]
                base[x, tile, y] = (
                    2.0 * center[tile] - earlier + courant[x, tile, y] * total[tile]
                )
        return 0

    lax.fori_loop(0, rows_x, step, 0, unroll=4)
    wait_all(copies)
    add_sources(
        base, cells_here, samples_here, wavelet_here, 1, rows_x, rows_y, depth
    )


def sides(first, second, even, at_first, at_last):
    low = jnp.where(even, second, first)
    high = jnp.where(even, first, second)
    return jnp.where(at_first, 0.0, low), jnp.where(at_last, 0.0, high)


def add_halos(base, courant, x_first, x_second, y_first, y_second, x_halo, y_halo, store):
    rows_x, tiles, rows_y, _ = base.shape
    y_tiles = rows_y // SUB
    even_x, first_x, last_x = parity("gx")
    even_y, first_y, last_y = parity("gy")
    lower = iota(0) < HALO
    zero = jnp.zeros((SUB, LANES), jnp.float32)
    for slot in range(HALO):
        for tile in range(tiles):
            for y_tile in range(y_tiles):
                y = pl.ds(y_tile * SUB, SUB)
                low, high = sides(
                    x_first[slot, tile, y], x_second[slot, tile, y], even_x, first_x, last_x
                )
                x_halo[slot, tile, y] = low
                x_halo[HALO + slot, tile, y] = high

    def spread(x, _):
        for pair in range(tiles // 2):
            low, high = sides(y_first[x, pair], y_second[x, pair], even_y, first_y, last_y)
            for half, tile in enumerate((2 * pair, 2 * pair + 1)):
                y_halo[x, tile, pl.ds(0, SUB)] = jnp.where(lower, rolled(low, half * HALO, 0), 0.0)
                y_halo[x, tile, pl.ds(SUB, SUB)] = zero
                y_halo[x, tile, pl.ds(2 * SUB, SUB)] = jnp.where(
                    lower, rolled(high, half * HALO, 0), 0.0
                )
        return 0

    lax.fori_loop(0, rows_x, spread, 0, unroll=4)

    def finish(x, x_terms):
        for y_tile in range(y_tiles):
            y = pl.ds(y_tile * SUB, SUB)
            done = []
            for tile in range(tiles):
                beyond = None
                terms = [(w, x_halo[slot, tile, y]) for w, slot in x_terms]
                for offset in range(1, HALO + 1):
                    weight = STENCIL_WEIGHTS[offset]
                    if y_tile == 0:
                        terms.append((weight, y_halo[x, tile, pl.ds(HALO - offset, SUB)]))
                    if y_tile == y_tiles - 1:
                        terms.append((weight, y_halo[x, tile, pl.ds(SUB + offset, SUB)]))
                for weight, value in terms:
                    beyond = weight * value if beyond is None else beyond + weight * value
                value = base[x, tile, y]
                if beyond is not None:
                    value = value + courant[x, tile, y] * beyond
                done.append(value)
            store(x, y_tile, done)

    for x in list(range(HALO)) + list(range(rows_x - HALO, rows_x)):
        x_terms = []
        for offset in range(1, HALO + 1):
            if x - offset < 0:
                x_terms.append((STENCIL_WEIGHTS[offset], HALO + x - offset))
            if x + offset >= rows_x:
                x_terms.append((STENCIL_WEIGHTS[offset], HALO + x + offset - rows_x))
        finish(x, x_terms)

    def inner(x, _):
        finish(x, ())
        return 0

    lax.fori_loop(HALO, rows_x - HALO, inner, 0, unroll=4)


def mid_kernel(
    base, courant, x_in, x_in_2, y_in, y_in_2, blank,
    padded, x_first, x_second, y_first, y_second, x_halo, y_halo,
):
    rows_x, tiles, rows_y, _ = base.shape
    even_x, _, _ = parity("gx")
    even_y, _, _ = parity("gy")

    def store(x, y_tile, values):
        for tile, value in enumerate(values):
            padded[x + HALO, tile, pl.ds(SUB + y_tile * SUB, SUB)] = value

    add_halos(base, courant, x_in, x_in_2, y_in, y_in_2, x_halo, y_halo, store)
    field = padded_vector(padded)
    pack_x(field, range(HALO), range(rows_x - HALO, rows_x), even_x, x_first, x_second)
    pack_y(field, rows_x, tiles, rows_y // SUB, even_y, y_first, y_second)


def lift_depth(values):
    lane = iota(1)
    odd = lax.rem(lane, 2) == 1
    tiles = len(values)
    for weight, on_odd in (
        (LIFT_ALPHA, True), (LIFT_BETA, False), (LIFT_GAMMA, True), (LIFT_DELTA, False)
    ):
        factor = jnp.where(odd if on_odd else ~odd, weight, 0.0)
        up = [rolled(value, -1, 1) for value in values]
        down = [rolled(value, 1, 1) for value in values]
        result = []
        for tile in range(tiles):
            above = up[tile + 1] if tile + 1 < tiles else down[tile]
            below = down[tile - 1] if tile else up[tile]
            beside = jnp.where(lane < LANES - 1, up[tile], above)
            beside = beside + jnp.where(lane >= 1, down[tile], below)
            result.append(values[tile] + factor * beside)
        values = result
    return values


def next_kernel(
    base, courant, x_in, x_in_2, y_in, y_in_2,
    field, x_first, x_second, x_halo, y_halo,
):
    rows_x, tiles, rows_y, _ = base.shape
    even_x, _, _ = parity("gx")

    def store(x, y_tile, values):
        y = pl.ds(y_tile * SUB, SUB)
        for tile, value in enumerate(values):
            field[x, tile, y] = value

    add_halos(base, courant, x_in, x_in_2, y_in, y_in_2, x_halo, y_halo, store)
    for tile in range(tiles):
        for y_tile in range(rows_y // SUB):
            y = pl.ds(y_tile * SUB, SUB)
            start = [field[x, tile, y] for x in range(3)]
            end = [field[x, tile, y] for x in range(rows_x - 4, rows_x)]
            low = (start[0], start[1] + LIFT_ALPHA * (start[0] + start[2]))
            high = (
                end[2] + LIFT_BETA * (end[1] + LIFT_ALPHA * (end[0] + end[2])),
                end[3] + LIFT_ALPHA * end[2],
            )
            for slot in range(2):
                x_first[slot, tile, y] = jnp.where(even_x, high[slot], low[slot])
                x_second[slot, tile, y] = jnp.where(even_x, low[slot], high[slot])


def outward(field, out, sems):
    tiles = field.shape[1]
    return paired(
        [field.at[:, tile] for tile in range(tiles)],
        [out.at[:, :, pl.ds(tile * LANES, LANES)] for tile in range(tiles)],
        sems,
    )


def lift_depth_all(source, target):
    rows_x, tiles, rows_y, _ = source.shape

    def step(x, _):
        for y_tile in range(rows_y // SUB):
            y = pl.ds(y_tile * SUB, SUB)
            lifted = lift_depth([source[x, tile, y] for tile in range(tiles)])
            for tile, value in enumerate(lifted):
                target[x, tile, y] = value
        return 0

    lax.fori_loop(0, rows_x, step, 0, unroll=min(4, rows_x))


def depth_kernel(field, lifted, out, sems):
    copies = start_all(outward(field, out, sems))
    lift_depth_all(field, lifted)
    wait_all(copies)


def lift_x_kernel(lifted, x_raw, x_raw_2, out, y_first, y_second, x_in, x_in_2):
    rows_x, tiles, rows_y, _ = lifted.shape
    y_tiles = rows_y // SUB
    half = rows_x // 2
    lift_depth_all(x_raw, x_in)
    lift_depth_all(x_raw_2, x_in_2)
    even_x, first_x, last_x = parity("gx")
    even_y, _, _ = parity("gy")

    def column(tile, _):
        for y_tile in range(y_tiles):
            y = pl.ds(y_tile * SUB, SUB)
            got = [
                (
                    jnp.where(even_x, x_in_2[slot, tile, y], x_in[slot, tile, y]),
                    jnp.where(even_x, x_in[slot, tile, y], x_in_2[slot, tile, y]),
                )
                for slot in range(2)
            ]
            even = [lifted[2 * i, tile, y] for i in range(half)]
            odd = [lifted[2 * i + 1, tile, y] for i in range(half)]
            beyond = jnp.where(last_x, even[-1], got[0][1])
            even.append(beyond)
            odd = [odd[i] + LIFT_ALPHA * (even[i] + even[i + 1]) for i in range(half)]
            before = got[1][0] + LIFT_ALPHA * even[0]
            odd = [jnp.where(first_x, odd[0], before)] + odd
            last = even.pop() + LIFT_BETA * (odd[-1] + got[1][1])
            even = [even[i] + LIFT_BETA * (odd[i] + odd[i + 1]) for i in range(half)]
            even.append(jnp.where(last_x, even[-1], last))
            start = got[0][0] + LIFT_BETA * odd[0]
            start = odd[0] + LIFT_GAMMA * (start + even[0])
            odd = [odd[i + 1] + LIFT_GAMMA * (even[i] + even[i + 1]) for i in range(half)]
            padded = [jnp.where(first_x, odd[0], start)] + odd
            even = [even[i] + LIFT_DELTA * (padded[i] + padded[i + 1]) for i in range(half)]
            for i in range(half):
                out[2 * i, tile, y] = even[i]
                out[2 * i + 1, tile, y] = odd[i]
        return 0

    lax.fori_loop(0, tiles, column, 0)
    sub = iota(0)
    per = SUB // 2

    def pack(x, _):
        for group in range(tiles // per):
            packed = [None, None]
            for place in range(per):
                tile = group * per + place
                start = out[x, tile, pl.ds(0, SUB)]
                end = out[x, tile, pl.ds((y_tiles - 1) * SUB, SUB)]
                beside = rolled(start, 1, 0) + rolled(start, -1, 0)
                low = jnp.where(sub == 0, start, start + LIFT_ALPHA * beside)
                below = rolled(end, 1, 0)
                odd = end + LIFT_ALPHA * (below + rolled(end, -1, 0))
                high = jnp.where(
                    sub == SUB - 1,
                    end + LIFT_ALPHA * below,
                    end + LIFT_BETA * rolled(odd, 1, 0),
                )
                high = rolled(high, 2, 0)
                picked = (jnp.where(even_y, high, low), jnp.where(even_y, low, high))
                for side in range(2):
                    value = rolled(picked[side], 2 * place, 0)
                    if place:
                        value = jnp.where(sub >= 2 * place, value, packed[side])
                    packed[side] = value
            y_first[x, group] = packed[0]
            y_second[x, group] = packed[1]
        return 0

    lax.fori_loop(0, rows_x, pack, 0, unroll=4)


def lift_y_kernel(lifted, y_in, y_in_2, out, codes, sems):
    rows_x, tiles, rows_y, _ = lifted.shape
    even_y, first_y, last_y = parity("gy")
    sub = iota(0)
    z_odd = lax.rem(iota(1), 2) == 1
    per = SUB // 2
    top = sub == SUB - 1
    bottom = sub == 0
    at_first = bottom & first_y
    at_last = top & last_y

    def scale(x_odd, y_odd):
        power = (1 if x_odd else -1) + (1 if y_odd else -1)
        return jnp.where(z_odd, LIFT_SCALE ** (power + 1), LIFT_SCALE ** (power - 1))

    def code(value):
        kept = jnp.maximum(value - DEAD_ZONE, 0.0) + jnp.minimum(value + DEAD_ZONE, 0.0)
        return kept * (1.0 / QUANT_STEP)

    def row(x, x_odd):
        for group in range(tiles // per):
            low = jnp.where(even_y, y_in_2[x, group], y_in[x, group])
            high = jnp.where(even_y, y_in[x, group], y_in_2[x, group])
            for place in range(per):
                tile = group * per + place
                even = lifted[x, tile, pl.ds(0, SUB, stride=2)]
                odd = lifted[x, tile, pl.ds(1, SUB, stride=2)]
                far = rolled(high, SUB - 1 - 2 * place, 0)
                far_odd = rolled(high, SUB - 2 - 2 * place, 0)
                near = rolled(low, -2 * place, 0)
                near_odd = rolled(low, -2 * place - 1, 0)
                beyond = jnp.where(at_last, even, jnp.where(top, far, rolled(even, -1, 0)))
                odd = odd + LIFT_ALPHA * (even + beyond)
                before = near_odd + LIFT_ALPHA * even
                under = jnp.where(at_first, odd, jnp.where(bottom, before, rolled(odd, 1, 0)))
                last = far + LIFT_BETA * (odd + far_odd)
                even = even + LIFT_BETA * (odd + under)
                beyond = jnp.where(at_last, even, jnp.where(top, last, rolled(even, -1, 0)))
                start = before + LIFT_GAMMA * (near + LIFT_BETA * before + even)
                odd = odd + LIFT_GAMMA * (even + beyond)
                under = jnp.where(at_first, odd, jnp.where(bottom, start, rolled(odd, 1, 0)))
                even = even + LIFT_DELTA * (odd + under)
                codes[x, tile, pl.ds(0, SUB, stride=2)] = code(even * scale(x_odd, False))
                codes[x, tile, pl.ds(1, SUB, stride=2)] = code(odd * scale(x_odd, True))

    def step(pair, _):
        row(2 * pair, False)
        row(2 * pair + 1, True)
        return 0

    lax.fori_loop(0, rows_x // 2, step, 0, unroll=2)
    wait_all(start_all(outward(codes, out, sems)))


def whole(count):
    return [pl.BlockSpec(memory_space=pltpu.VMEM)] * count


def scalars(count):
    return [pl.BlockSpec(memory_space=pltpu.SMEM)] * count


def far(count):
    return [pl.BlockSpec(memory_space=pltpu.HBM)] * count


def call(kernel, in_specs, out_specs, out_shape, scratch=(), cost=1.0, aliases=None, **kwargs):
    return pl.pallas_call(
        kernel,
        in_specs=in_specs,
        out_specs=out_specs,
        out_shape=[jax.ShapeDtypeStruct(shape, jnp.float32) for shape in out_shape],
        scratch_shapes=list(scratch),
        input_output_aliases=aliases or {},
        compiler_params=pltpu.CompilerParams(vmem_limit_bytes=16 << 20),
        cost_estimate=pl.CostEstimate(
            flops=int(cost * 1e6), bytes_accessed=int(cost * 1e6), transcendentals=0
        ),
        **kwargs,
    )


def swaps(names, counts, partner):
    pairs = []
    for y in range(counts[0]):
        for x in range(counts[1]):
            target = partner(y, x)
            pairs.append((y * counts[1] + x, target[0] * counts[1] + target[1]))
    return functools.partial(lax.ppermute, axis_name=names, perm=pairs)


def exchanges(count_y, count_x):
    names = ("gy", "gx")
    counts = (count_y, count_x)

    def second(index, count):
        return (index + 1) % count if index % 2 else (index - 1) % count

    x_first = swaps(names, counts, lambda y, x: (y, x ^ 1))
    x_second = swaps(names, counts, lambda y, x: (y, second(x, count_x)))
    y_first = swaps(names, counts, lambda y, x: (y ^ 1, x))

    def inner_y(y, x):
        return (second(y, count_y), x) if 0 < y < count_y - 1 else (y, x ^ 1)

    return x_first, x_second, y_first, swaps(names, counts, inner_y)


def shards(pressure_now, pressure_old, classes, class_table, wavelet, source_cells, samples):
    rows_x, rows_y, depth = pressure_now.shape
    tiles = depth // LANES
    swap_x, swap_x_2, swap_y, swap_y_2 = exchanges(lax.axis_size("gy"), lax.axis_size("gx"))
    padded_shape = (rows_x + 2 * HALO, tiles, rows_y + 2 * SUB, LANES)
    block_shape = (rows_x, tiles, rows_y, LANES)
    x_shape = (HALO, tiles, rows_y, LANES)
    y_shape = (rows_x, tiles // 2, SUB, LANES)
    x_lift_shape = (2, tiles, rows_y, LANES)
    y_lift_shape = (rows_x, tiles // 4, SUB, LANES)
    natural = (rows_x, rows_y, depth)
    sems = pltpu.SemaphoreType.DMA((tiles,))
    halos = (
        pltpu.VMEM((2 * HALO, tiles, rows_y, LANES), jnp.float32),
        pltpu.VMEM((rows_x, tiles, 3 * SUB, LANES), jnp.float32),
    )

    def star(sends):
        x_1, x_2, y_1, y_2 = sends
        got_y, got_y_2 = swap_y(y_1), swap_y_2(y_2)
        got_x_2, got_x = swap_x_2(x_2), swap_x(x_1)
        return got_x, got_x_2, got_y, got_y_2

    f32 = jnp.float32
    scalar_memory = (
        pltpu.SMEM(wavelet.shape, f32),
        pltpu.SMEM(source_cells.shape, jnp.int32),
        pltpu.SMEM(samples.shape, jnp.int32),
    )
    pressure_old, classes, class_table, wavelet, source_cells, samples = (
        pltpu.with_memory_space_constraint(array, pltpu.HBM)
        for array in (pressure_old, classes, class_table, wavelet, source_cells, samples)
    )
    sends = call(
        sends_kernel, whole(1), whole(4), [x_shape, x_shape, y_shape, y_shape], name="sends"
    )(pressure_now)
    got = star(sends)
    now, base, courant, blank = call(
        first_local_kernel, whole(1) + far(6), whole(4),
        [padded_shape, block_shape, block_shape, padded_shape],
        (
            pltpu.VMEM(natural, f32), pltpu.VMEM(natural, jnp.int32),
            pltpu.SMEM(class_table.shape, f32), *scalar_memory,
            pltpu.SemaphoreType.DMA((6,)),
        ),
        cost=4.0, name="first_local",
    )(pressure_now, pressure_old, classes, class_table, wavelet, source_cells, samples)
    mid, *sends = call(
        mid_kernel, whole(7), whole(5), [padded_shape, x_shape, x_shape, y_shape, y_shape],
        halos, aliases={6: 0}, name="mid",
    )(base, courant, *got, blank)
    got = star(sends)
    base, pressure_mid = call(
        second_local_kernel, whole(3) + far(3), whole(1) + far(1), [block_shape, natural],
        (*scalar_memory, pltpu.SemaphoreType.DMA((tiles + 3,))), cost=4.0, name="second_local",
    )(mid, now, courant, wavelet, source_cells, samples)
    field, *sends = call(
        next_kernel, whole(6), whole(3), [block_shape, x_lift_shape, x_lift_shape],
        halos, name="next",
    )(base, courant, *got)
    got_2, got = swap_x_2(sends[1]), swap_x(sends[0])
    lifted, pressure_next = call(
        depth_kernel, whole(1), whole(1) + far(1), [block_shape, natural], (sems,), cost=4.0,
        name="depth",
    )(field)
    lifted, *sends = call(
        lift_x_kernel, whole(3), whole(3), [block_shape, y_lift_shape, y_lift_shape],
        (pltpu.VMEM(x_lift_shape, f32), pltpu.VMEM(x_lift_shape, f32)), name="lift_x",
    )(lifted, got, got_2)
    got, got_2 = swap_y(sends[0]), swap_y_2(sends[1])
    (snapshot_code,) = call(
        lift_y_kernel, whole(3), far(1), [natural],
        (pltpu.VMEM(block_shape, f32), sems), name="lift_y",
    )(lifted, got, got_2)
    return (pressure_next, pressure_mid, snapshot_code)


def solution(mesh):
    block = P(("shot", "gx"), "gy", None)
    return jax.shard_map(
        shards,
        mesh=mesh,
        in_specs=(block, block, block, P(), P("shot"), P("shot"), P("shot")),
        out_specs=(block, block, block),
        check_vma=False,
    )
```

```python
import functools

import jax
import jax.numpy as jnp
from jax import lax
from jax.experimental import pallas as pl
from jax.experimental.pallas import tpu as pltpu
from jax.sharding import PartitionSpec as P


STENCIL_WEIGHTS = (-205.0 / 72.0, 8.0 / 5.0, -1.0 / 5.0, 8.0 / 315.0, -1.0 / 560.0)
LIFT_ALPHA = -1.586134342
LIFT_BETA = -0.05298011854
LIFT_GAMMA = 0.8829110762
LIFT_DELTA = 0.4435068522
LIFT_SCALE = 1.149604398
DEAD_ZONE = 0.25
QUANT_STEP = 0.5

HALO = 4
LANES = 128
SUB = 8


def iota(axis):
    return lax.broadcasted_iota(jnp.int32, (SUB, LANES), axis)


def rolled(value, shift, axis):
    size = value.shape[axis]
    shift = shift % size
    return value if shift == 0 else pltpu.roll(value, shift, axis)


def parity(axis):
    index = lax.axis_index(axis)
    return lax.rem(index, 2) == 0, index == 0, index == lax.axis_size(axis) - 1


def pack_x(field, low, high, even, x_first, x_second):
    for slot, (down, up) in enumerate(zip(low, high)):
        for tile in range(x_first.shape[1]):
            for y_tile in range(x_first.shape[2] // SUB):
                below, above = field(down, tile, y_tile), field(up, tile, y_tile)
                where = (slot, tile, pl.ds(y_tile * SUB, SUB))
                x_first[where] = jnp.where(even, above, below)
                x_second[where] = jnp.where(even, below, above)


def pack_y(rows, rows_x, tiles, even, y_first, y_second):
    def step(x, _):
        for tile in range(tiles):
            below, above = rows(x, tile)
            where = (x, tile // 2, pl.ds(tile % 2 * HALO, HALO))
            y_first[where] = jnp.where(even, above, below)
            y_second[where] = jnp.where(even, below, above)
        return 0

    lax.fori_loop(0, rows_x, step, 0, unroll=4)


def zero_pads(padded, rows_x, rows_y):
    zero = jnp.zeros((SUB, LANES), jnp.float32)
    tiles = padded.shape[1]
    for x in list(range(HALO)) + list(range(rows_x + HALO, rows_x + 2 * HALO)):
        for tile in range(tiles):
            for y in range(SUB, rows_y + SUB, SUB):
                padded[x, tile, pl.ds(y, SUB)] = zero

    def step(x, _):
        for tile in range(tiles):
            padded[x + HALO, tile, pl.ds(0, SUB)] = zero
            padded[x + HALO, tile, pl.ds(rows_y + SUB, SUB)] = zero
        return 0

    lax.fori_loop(0, rows_x, step, 0)


def padded_vector(padded):
    return lambda x, tile, y_tile: padded[x + HALO, tile, pl.ds(SUB + y_tile * SUB, SUB)]


def sends_kernel(now, x_first, x_second, y_first, y_second):
    rows_x, rows_y, depth = now.shape
    even_x, _, _ = parity("gx")
    even_y, _, _ = parity("gy")

    def field(x, tile, y_tile):
        return now[x, pl.ds(y_tile * SUB, SUB), pl.ds(tile * LANES, LANES)]

    pack_x(field, range(HALO), range(rows_x - HALO, rows_x), even_x, x_first, x_second)

    def rows(x, tile):
        z = pl.ds(tile * LANES, LANES)
        return now[x, pl.ds(0, HALO), z], now[x, pl.ds(rows_y - HALO, HALO), z]

    pack_y(rows, rows_x, depth // LANES, even_y, y_first, y_second)


def local_laplace(padded, x, tiles, y_tile):
    lane = iota(1)
    row, y = x + HALO, SUB + y_tile * SUB
    center = [padded[row, tile, pl.ds(y, SUB)] for tile in range(tiles)]
    zero = jnp.zeros((SUB, LANES), jnp.float32)
    total = [3.0 * STENCIL_WEIGHTS[0] * value for value in center]
    for offset in range(1, HALO + 1):
        up = [rolled(value, -offset, 1) for value in center] + [zero]
        down = [zero] + [rolled(value, offset, 1) for value in center]
        for tile in range(tiles):
            beside = jnp.where(lane < LANES - offset, up[tile], up[tile + 1])
            beside = beside + jnp.where(lane >= offset, down[tile + 1], down[tile])
            beside = beside + (
                padded[row + offset, tile, pl.ds(y, SUB)]
                + padded[row - offset, tile, pl.ds(y, SUB)]
            )
            beside = beside + (
                padded[row, tile, pl.ds(y + offset, SUB)]
                + padded[row, tile, pl.ds(y - offset, SUB)]
            )
            total[tile] = total[tile] + STENCIL_WEIGHTS[offset] * beside
    return center, total


def add_sources(base, cells, samples, wavelet, step_index, rows_x, rows_y, depth):
    all_y = rows_y * lax.axis_size("gy")
    start_x = lax.axis_index("gx") * rows_x
    start_y = lax.axis_index("gy") * rows_y
    lane = lax.broadcasted_iota(jnp.int32, (1, LANES), 1)
    for shot in range(cells.shape[0]):
        cell = cells[shot]
        x = lax.div(cell, all_y * depth) - start_x
        y = lax.rem(lax.div(cell, depth), all_y) - start_y
        z = lax.rem(cell, depth)
        inside = (x >= 0) & (x < rows_x) & (y >= 0) & (y < rows_y)

        @pl.when(inside)
        def _():
            value = wavelet[lax.rem(samples[shot] + step_index, wavelet.shape[0])]
            where = (x, lax.div(z, LANES), pl.ds(y, 1))
            base[where] = base[where] + jnp.where(lane == lax.rem(z, LANES), value, 0.0)


def start_all(copies):
    for copy in copies:
        copy.start()
    return copies


def wait_all(copies):
    for copy in copies:
        copy.wait()


def paired(sources, targets, sems):
    return [
        pltpu.make_async_copy(source, target, sems.at[place])
        for place, (source, target) in enumerate(zip(sources, targets))
    ]


def first_local_kernel(
    now, old, classes, table, wavelet, cells, samples,
    padded, base, courant, blank,
    old_here, classes_here, table_here, wavelet_here, cells_here, samples_here, sems,
):
    rows_x, rows_y, depth = old.shape
    tiles = depth // LANES
    lane = iota(1)
    copies = start_all(
        paired(
            (table, classes, old, wavelet, cells, samples),
            (table_here, classes_here, old_here, wavelet_here, cells_here, samples_here),
            sems,
        )
    )
    zero_pads(padded, rows_x, rows_y)

    def spread(x, _):
        for tile in range(tiles):
            for y in range(0, rows_y, SUB):
                padded[x + HALO, tile, pl.ds(SUB + y, SUB)] = now[
                    x, pl.ds(y, SUB), pl.ds(tile * LANES, LANES)
                ]
        return 0

    lax.fori_loop(0, rows_x, spread, 0, unroll=4)

    def sums(x, _):
        for y_tile in range(rows_y // SUB):
            _, total = local_laplace(padded, x, tiles, y_tile)
            for tile in range(tiles):
                base[x, tile, pl.ds(y_tile * SUB, SUB)] = total[tile]
        return 0

    lax.fori_loop(0, rows_x, sums, 0, unroll=4)
    wait_all(copies)
    entries = jnp.zeros((SUB, LANES), jnp.float32)
    for material in range(table.shape[0]):
        entries = jnp.where(lane == material, table_here[material], entries)

    def step(x, _):
        for y_tile in range(rows_y // SUB):
            y = pl.ds(y_tile * SUB, SUB)
            for tile in range(tiles):
                z = pl.ds(tile * LANES, LANES)
                speed = jnp.take_along_axis(entries, classes_here[x, y, z], axis=1)
                courant[x, tile, y] = speed
                base[x, tile, y] = (
                    2.0 * now[x, y, z] - old_here[x, y, z] + speed * base[x, tile, y]
                )
        return 0

    lax.fori_loop(0, rows_x, step, 0, unroll=4)
    add_sources(
        base, cells_here, samples_here, wavelet_here, 0, rows_x, rows_y, depth
    )
    zero_pads(blank, rows_x, rows_y)


def second_local_kernel(
    padded, before, courant, wavelet, cells, samples,
    base, mid,
    wavelet_here, cells_here, samples_here, sems,
):
    rows_x, rows_y, depth = mid.shape
    tiles = depth // LANES
    copies = start_all(
        paired(
            [wavelet, cells, samples]
            + [padded.at[pl.ds(HALO, rows_x), t, pl.ds(SUB, rows_y), :] for t in range(tiles)],
            [wavelet_here, cells_here, samples_here]
            + [mid.at[:, :, pl.ds(t * LANES, LANES)] for t in range(tiles)],
            sems,
        )
    )

    def step(x, _):
        for y_tile in range(rows_y // SUB):
            center, total = local_laplace(padded, x, tiles, y_tile)
            y = pl.ds(y_tile * SUB, SUB)
            for tile in range(tiles):
                earlier = before[x + HALO, tile, pl.ds(SUB + y_tile * SUB, SUB)]
                base[x, tile, y] = (
                    2.0 * center[tile] - earlier + courant[x, tile, y] * total[tile]
                )
        return 0

    lax.fori_loop(0, rows_x, step, 0, unroll=4)
    wait_all(copies)
    add_sources(
        base, cells_here, samples_here, wavelet_here, 1, rows_x, rows_y, depth
    )


def sides(first, second, even, at_first, at_last):
    low = jnp.where(even, second, first)
    high = jnp.where(even, first, second)
    return jnp.where(at_first, 0.0, low), jnp.where(at_last, 0.0, high)


def add_halos(base, courant, x_first, x_second, y_first, y_second, x_halo, y_halo, rows, store):
    rows_x, tiles, rows_y, _ = base.shape
    y_tiles = rows_y // SUB
    even_x, first_x, last_x = parity("gx")
    even_y, first_y, last_y = parity("gy")
    zero = jnp.zeros((SUB, LANES), jnp.float32)
    for slot in range(HALO if x_halo is not None else 0):
        for tile in range(tiles):
            for y_tile in range(y_tiles):
                y = pl.ds(y_tile * SUB, SUB)
                low, high = sides(
                    x_first[slot, tile, y], x_second[slot, tile, y], even_x, first_x, last_x
                )
                x_halo[slot, tile, y] = low
                x_halo[HALO + slot, tile, y] = high

    def spread(x):
        for tile in range(tiles):
            where = (x, tile // 2, pl.ds(tile % 2 * HALO, HALO))
            low, high = sides(y_first[where], y_second[where], even_y, first_y, last_y)
            y_halo[x, tile, pl.ds(HALO, SUB)] = zero
            y_halo[x, tile, pl.ds(SUB, SUB)] = zero
            y_halo[x, tile, pl.ds(0, HALO)] = low
            y_halo[x, tile, pl.ds(2 * SUB, HALO)] = high

    def finish(x, x_terms):
        for y_tile in range(y_tiles):
            y = pl.ds(y_tile * SUB, SUB)
            done = []
            for tile in range(tiles):
                beyond = None
                terms = [(w, x_halo[slot, tile, y]) for w, slot in x_terms]
                for offset in range(1, HALO + 1):
                    weight = STENCIL_WEIGHTS[offset]
                    if y_tile == 0:
                        terms.append((weight, y_halo[x, tile, pl.ds(HALO - offset, SUB)]))
                    if y_tile == y_tiles - 1:
                        terms.append((weight, y_halo[x, tile, pl.ds(SUB + offset, SUB)]))
                for weight, value in terms:
                    beyond = weight * value if beyond is None else beyond + weight * value
                value = base[x, tile, y]
                if beyond is not None:
                    value = value + courant[x, tile, y] * beyond
                done.append(value)
            store(x, y_tile, done)

    for x in rows:
        spread(x)
    for x in rows:
        x_terms = []
        for offset in range(1, HALO + 1):
            if x - offset < 0:
                x_terms.append((STENCIL_WEIGHTS[offset], HALO + x - offset))
            if x + offset >= rows_x:
                x_terms.append((STENCIL_WEIGHTS[offset], HALO + x + offset - rows_x))
        finish(x, x_terms)


def inner_rows(rows_x):
    return range(HALO, rows_x - HALO)


def outer_rows(rows_x):
    return [*range(HALO), *range(rows_x - HALO, rows_x)]


def mid_kernel(
    base, courant, x_in, x_in_2, y_in, y_in_2, blank,
    padded, x_first, x_second, y_first, y_second, x_halo, y_halo,
):
    rows_x, tiles, rows_y, _ = base.shape
    even_x, _, _ = parity("gx")
    even_y, _, _ = parity("gy")

    def store(x, y_tile, values):
        for tile, value in enumerate(values):
            padded[x + HALO, tile, pl.ds(SUB + y_tile * SUB, SUB)] = value

    add_halos(
        base, courant, x_in, x_in_2, y_in, y_in_2, x_halo, y_halo, range(rows_x), store
    )
    field = padded_vector(padded)
    pack_x(field, range(HALO), range(rows_x - HALO, rows_x), even_x, x_first, x_second)

    def rows(x, tile):
        y = SUB + rows_y - HALO
        return padded[x + HALO, tile, pl.ds(SUB, HALO)], padded[x + HALO, tile, pl.ds(y, HALO)]

    pack_y(rows, rows_x, tiles, even_y, y_first, y_second)


def lift_depth(first, second):
    lane = iota(1)
    early = lax.rem(lane, 2) == 0
    tiles = range(len(first))
    even = [jnp.where(early, a, rolled(b, 1, 1)) for a, b in zip(first, second)]
    odd = [jnp.where(early, rolled(a, -1, 1), b) for a, b in zip(first, second)]
    for weight_odd, weight_even in ((LIFT_ALPHA, LIFT_BETA), (LIFT_GAMMA, LIFT_DELTA)):
        up = [rolled(value, -2, 1) for value in even]
        up.append(even[-1])
        above = [jnp.where(lane < LANES - 2, up[t], up[t + 1]) for t in tiles]
        odd = [odd[t] + weight_odd * (even[t] + above[t]) for t in tiles]
        down = [odd[0]] + [rolled(value, 2, 1) for value in odd]
        below = [jnp.where(lane >= 2, down[t + 1], down[t]) for t in tiles]
        even = [even[t] + weight_even * (odd[t] + below[t]) for t in tiles]
    return (
        [jnp.where(early, e, rolled(o, 1, 1)) for e, o in zip(even, odd)],
        [jnp.where(early, rolled(e, -1, 1), o) for e, o in zip(even, odd)],
    )


def next_kernel(
    base, courant, x_in, x_in_2, y_in, y_in_2,
    field, x_first, x_second, x_halo, y_halo,
):
    rows_x, tiles, rows_y, _ = base.shape
    even_x, _, _ = parity("gx")

    def store(x, y_tile, values):
        y = pl.ds(y_tile * SUB, SUB)
        for tile, value in enumerate(values):
            field[x, tile, y] = value

    add_halos(
        base, courant, x_in, x_in_2, y_in, y_in_2, x_halo, y_halo, outer_rows(rows_x), store
    )
    for y_tile in range(rows_y // SUB):
        y = pl.ds(y_tile * SUB, SUB)
        rows = []
        for tile in range(tiles):
            start = [field[x, tile, y] for x in range(3)]
            end = [field[x, tile, y] for x in range(rows_x - 4, rows_x)]
            low = (start[0], start[1] + LIFT_ALPHA * (start[0] + start[2]))
            high = (
                end[2] + LIFT_BETA * (end[1] + LIFT_ALPHA * (end[0] + end[2])),
                end[3] + LIFT_ALPHA * end[2],
            )
            rows.append(low + high)
        for slot in range(2):
            low, high = lift_depth(
                [row[slot] for row in rows], [row[2 + slot] for row in rows]
            )
            for tile in range(tiles):
                x_first[slot, tile, y] = jnp.where(even_x, high[tile], low[tile])
                x_second[slot, tile, y] = jnp.where(even_x, low[tile], high[tile])


def outward(field, out, sems):
    tiles = field.shape[1]
    return paired(
        [field.at[:, tile] for tile in range(tiles)],
        [out.at[:, :, pl.ds(tile * LANES, LANES)] for tile in range(tiles)],
        sems,
    )


def depth_kernel(base, courant, y_in, y_in_2, edges, field, lifted, out, y_halo, sems):
    rows_x, tiles, rows_y, _ = base.shape

    def store(x, y_tile, values):
        for tile, value in enumerate(values):
            field[x, tile, pl.ds(y_tile * SUB, SUB)] = value

    add_halos(
        base, courant, None, None, y_in, y_in_2, None, y_halo, inner_rows(rows_x), store
    )
    copies = start_all(outward(field, out, sems))

    def step(x, _):
        for y in range(0, rows_y, 2 * SUB):
            here = pl.ds(y, SUB), pl.ds(y + SUB, SUB)
            pair = lift_depth(
                *([field[x, tile, part] for tile in range(tiles)] for part in here)
            )
            for part, values in zip(here, pair):
                for tile, value in enumerate(values):
                    lifted[x, tile, part] = value
        return 0

    lax.fori_loop(0, rows_x, step, 0, unroll=4)
    wait_all(copies)


def lift_x_kernel(lifted, x_in, x_in_2, out, y_first, y_second):
    rows_x, tiles, rows_y, _ = lifted.shape
    y_tiles = rows_y // SUB
    half = rows_x // 2
    even_x, first_x, last_x = parity("gx")
    even_y, _, _ = parity("gy")

    for tile in range(tiles):
        for y_tile in range(y_tiles):
            y = pl.ds(y_tile * SUB, SUB)
            got = [
                (
                    jnp.where(even_x, x_in_2[slot, tile, y], x_in[slot, tile, y]),
                    jnp.where(even_x, x_in[slot, tile, y], x_in_2[slot, tile, y]),
                )
                for slot in range(2)
            ]
            even = [lifted[2 * i, tile, y] for i in range(half)]
            odd = [lifted[2 * i + 1, tile, y] for i in range(half)]
            beyond = jnp.where(last_x, even[-1], got[0][1])
            even.append(beyond)
            odd = [odd[i] + LIFT_ALPHA * (even[i] + even[i + 1]) for i in range(half)]
            before = got[1][0] + LIFT_ALPHA * even[0]
            odd = [jnp.where(first_x, odd[0], before)] + odd
            last = even.pop() + LIFT_BETA * (odd[-1] + got[1][1])
            even = [even[i] + LIFT_BETA * (odd[i] + odd[i + 1]) for i in range(half)]
            even.append(jnp.where(last_x, even[-1], last))
            start = got[0][0] + LIFT_BETA * odd[0]
            start = odd[0] + LIFT_GAMMA * (start + even[0])
            odd = [odd[i + 1] + LIFT_GAMMA * (even[i] + even[i + 1]) for i in range(half)]
            padded = [jnp.where(first_x, odd[0], start)] + odd
            even = [even[i] + LIFT_DELTA * (padded[i] + padded[i + 1]) for i in range(half)]
            here = pl.ds(SUB + y_tile * SUB, SUB)
            for i in range(half):
                out[2 * i, tile, here] = even[i]
                out[2 * i + 1, tile, here] = odd[i]

    head = lax.broadcasted_iota(jnp.int32, (2, LANES), 0) == 0

    def pack(x, _):
        for tile in range(tiles):

            def rows(y):
                return out[x, tile, pl.ds(SUB + y, 2)]

            low = rows(0)
            low = low + jnp.where(head, 0.0, LIFT_ALPHA * (rows(-1) + rows(1)))
            end = rows_y - 2
            high, below = rows(end), rows(end - 1)
            more = LIFT_BETA * (below + LIFT_ALPHA * (rows(end - 2) + high))
            high = high + jnp.where(head, more, LIFT_ALPHA * below)
            where = (x, tile // 4, pl.ds(tile % 4 * 2, 2))
            y_first[where] = jnp.where(even_y, high, low)
            y_second[where] = jnp.where(even_y, low, high)
        return 0

    lax.fori_loop(0, rows_x, pack, 0, unroll=8)


def y_scales():
    z_odd = lax.rem(iota(1), 2) == 1

    def scale(x_odd, y_odd):
        power = (1 if x_odd else -1) + (1 if y_odd else -1)
        return jnp.where(
            z_odd, LIFT_SCALE ** (power + 1) / QUANT_STEP, LIFT_SCALE ** (power - 1) / QUANT_STEP
        )

    return [[scale(x_odd, y_odd) for y_odd in (False, True)] for x_odd in (False, True)]


def lift_y_local_kernel(lifted, even_out, odd_out):
    rows_x, tiles, _, _ = lifted.shape
    _, first_y, last_y = parity("gy")
    sub = iota(0)
    top = sub == SUB - 1
    bottom = sub == 0
    at_first = bottom & first_y
    at_last = top & last_y
    scales = y_scales()

    def row(x, x_odd):
        for tile in range(tiles):
            even = lifted[x, tile, pl.ds(SUB, SUB, stride=2)]
            odd = lifted[x, tile, pl.ds(SUB + 1, SUB, stride=2)]
            beyond = jnp.where(at_last, even, jnp.where(top, 0.0, rolled(even, -1, 0)))
            odd = odd + LIFT_ALPHA * (even + beyond)
            before = LIFT_ALPHA * even
            under = jnp.where(at_first, odd, jnp.where(bottom, before, rolled(odd, 1, 0)))
            last = LIFT_BETA * odd
            even = even + LIFT_BETA * (odd + under)
            beyond = jnp.where(at_last, even, jnp.where(top, last, rolled(even, -1, 0)))
            start = before + LIFT_GAMMA * (LIFT_BETA * before + even)
            odd = odd + LIFT_GAMMA * (even + beyond)
            under = jnp.where(at_first, odd, jnp.where(bottom, start, rolled(odd, 1, 0)))
            even = even + LIFT_DELTA * (odd + under)
            even_out[x, tile] = even * scales[x_odd][0]
            odd_out[x, tile] = odd * scales[x_odd][1]

    def step(pair, _):
        row(2 * pair, 0)
        row(2 * pair + 1, 1)
        return 0

    lax.fori_loop(0, rows_x // 2, step, 0, unroll=2)


def lift_y_kernel(even_in, odd_in, y_in, y_in_2, out, codes, sems):
    rows_x, tiles, _, _ = even_in.shape
    even_y, first_y, last_y = parity("gy")
    sub = iota(0)
    edge = DEAD_ZONE / QUANT_STEP
    a, b, g, d = LIFT_ALPHA, LIFT_BETA, LIFT_GAMMA, LIFT_DELTA

    def at(places, keep):
        total = jnp.zeros((SUB, LANES), jnp.float32)
        for place, weight in places.items():
            total = jnp.where(sub == place, weight, total)
        return jnp.where(keep, total, 0.0)

    last = SUB - 1
    low = (
        (at({0: d * g}, ~first_y), at({}, ~first_y)),
        (
            at({0: b + d * (1.0 + 3.0 * g * b), 1: d * g * b}, ~first_y),
            at({0: g * b}, ~first_y),
        ),
    )
    far_odd = a + g * (1.0 + 2.0 * b * a)
    high = (
        (
            at({last: b * a + d * (g * b * a + far_odd), last - 1: d * g * b * a}, ~last_y),
            at({last: far_odd, last - 1: g * b * a}, ~last_y),
        ),
        (at({last: d * g * b}, ~last_y), at({last: g * b}, ~last_y)),
    )
    scales = y_scales()
    weights = [
        [
            [
                tuple(
                    jnp.where(even_y, one[slot][part], other[slot][part]) * scales[x_odd][part]
                    for part in range(2)
                )
                for slot in range(2)
            ]
            for one, other in ((high, low), (low, high))
        ]
        for x_odd in range(2)
    ]

    def code(value):
        return value - jnp.minimum(jnp.maximum(value, -edge), edge)

    def row(x, x_odd):
        for tile in range(tiles):
            even, odd = even_in[x, tile], odd_in[x, tile]
            for message, own in zip((y_in, y_in_2), weights[x_odd]):
                for slot in range(2):
                    place = pl.ds(tile % 4 * 2 + slot, 1)
                    value = jnp.broadcast_to(message[x, tile // 4, place], (SUB, LANES))
                    even = even + own[slot][0] * value
                    odd = odd + own[slot][1] * value
            codes[x, tile, pl.ds(0, SUB, stride=2)] = code(even)
            codes[x, tile, pl.ds(1, SUB, stride=2)] = code(odd)

    chunk = rows_x // 4
    copies = [
        [
            pltpu.make_async_copy(
                codes.at[pl.ds(part * chunk, chunk), tile],
                out.at[pl.ds(part * chunk, chunk), :, pl.ds(tile * LANES, LANES)],
                sems.at[part, tile],
            )
            for tile in range(tiles)
        ]
        for part in range(4)
    ]
    for part in range(4):
        for x in range(part * chunk, (part + 1) * chunk):
            row(x, x % 2)
        start_all(copies[part])
    for part in copies:
        wait_all(part)


def whole(count):
    return [pl.BlockSpec(memory_space=pltpu.VMEM)] * count


def far(count):
    return [pl.BlockSpec(memory_space=pltpu.HBM)] * count


def call(kernel, in_specs, out_specs, out_shape, scratch=(), cost=1.0, aliases=None, **kwargs):
    return pl.pallas_call(
        kernel,
        in_specs=in_specs,
        out_specs=out_specs,
        out_shape=[jax.ShapeDtypeStruct(shape, jnp.float32) for shape in out_shape],
        scratch_shapes=list(scratch),
        input_output_aliases=aliases or {},
        compiler_params=pltpu.CompilerParams(vmem_limit_bytes=16 << 20),
        cost_estimate=pl.CostEstimate(
            flops=int(cost * 1e6), bytes_accessed=int(cost * 1e6), transcendentals=0
        ),
        **kwargs,
    )


def swaps(names, counts, partner):
    pairs = []
    for y in range(counts[0]):
        for x in range(counts[1]):
            target = partner(y, x)
            pairs.append((y * counts[1] + x, target[0] * counts[1] + target[1]))
    return functools.partial(lax.ppermute, axis_name=names, perm=pairs)


def exchanges(count_y, count_x):
    names = ("gy", "gx")
    counts = (count_y, count_x)

    def second(index, count):
        return (index + 1) % count if index % 2 else (index - 1) % count

    x_first = swaps(names, counts, lambda y, x: (y, x ^ 1))
    x_second = swaps(names, counts, lambda y, x: (y, second(x, count_x)))
    y_first = swaps(names, counts, lambda y, x: (y ^ 1, x))

    def inner_y(y, x):
        return (second(y, count_y), x) if 0 < y < count_y - 1 else (y, x ^ 1)

    return x_first, x_second, y_first, swaps(names, counts, inner_y)


def shards(pressure_now, pressure_old, classes, class_table, wavelet, source_cells, samples):
    rows_x, rows_y, depth = pressure_now.shape
    tiles = depth // LANES
    swap_x, swap_x_2, swap_y, swap_y_2 = exchanges(lax.axis_size("gy"), lax.axis_size("gx"))
    padded_shape = (rows_x + 2 * HALO, tiles, rows_y + 2 * SUB, LANES)
    block_shape = (rows_x, tiles, rows_y, LANES)
    x_shape = (HALO, tiles, rows_y, LANES)
    y_shape = (rows_x, tiles // 2, SUB, LANES)
    x_lift_shape = (2, tiles, rows_y, LANES)
    y_lift_shape = (rows_x, tiles // 4, SUB, LANES)
    tall_shape = (rows_x, tiles, rows_y + 2 * SUB, LANES)
    half_shape = (rows_x, tiles, rows_y // 2, LANES)
    natural = (rows_x, rows_y, depth)
    sems = pltpu.SemaphoreType.DMA((tiles,))
    halos = (
        pltpu.VMEM((2 * HALO, tiles, rows_y, LANES), jnp.float32),
        pltpu.VMEM((rows_x, tiles, 3 * SUB, LANES), jnp.float32),
    )

    def star(sends):
        got = []
        for place, swap in enumerate((swap_x, swap_x_2, swap_y, swap_y_2)):
            got.append(swap(sends[place]))
        return got

    f32 = jnp.float32
    scalar_memory = (
        pltpu.SMEM(wavelet.shape, f32),
        pltpu.SMEM(source_cells.shape, jnp.int32),
        pltpu.SMEM(samples.shape, jnp.int32),
    )
    pressure_old, classes, class_table, wavelet, source_cells, samples = (
        pltpu.with_memory_space_constraint(array, pltpu.HBM)
        for array in (pressure_old, classes, class_table, wavelet, source_cells, samples)
    )
    sends = call(
        sends_kernel, whole(1), whole(4), [x_shape, x_shape, y_shape, y_shape], name="sends"
    )(pressure_now)
    got = star(sends)
    now, base, courant, blank = call(
        first_local_kernel, whole(1) + far(6), whole(4),
        [padded_shape, block_shape, block_shape, padded_shape],
        (
            pltpu.VMEM(natural, f32), pltpu.VMEM(natural, jnp.int32),
            pltpu.SMEM(class_table.shape, f32), *scalar_memory,
            pltpu.SemaphoreType.DMA((6,)),
        ),
        cost=4.0, name="first_local",
    )(pressure_now, pressure_old, classes, class_table, wavelet, source_cells, samples)
    mid, *sends = call(
        mid_kernel, whole(7), whole(5), [padded_shape, x_shape, x_shape, y_shape, y_shape],
        halos, aliases={6: 0}, name="mid",
    )(base, courant, *got, blank)
    got = star(sends)
    base, pressure_mid = call(
        second_local_kernel, whole(3) + far(3), whole(1) + far(1), [block_shape, natural],
        (*scalar_memory, pltpu.SemaphoreType.DMA((tiles + 3,))), cost=4.0, name="second_local",
    )(mid, now, courant, wavelet, source_cells, samples)
    field, *sends = call(
        next_kernel, whole(6), whole(3), [block_shape, x_lift_shape, x_lift_shape],
        halos, name="next",
    )(base, courant, *got)
    got_y = got[2:]
    got_2, got = swap_x_2(sends[1]), swap_x(sends[0])
    _, lifted, pressure_next = call(
        depth_kernel, whole(5), whole(2) + far(1), [block_shape, block_shape, natural],
        (halos[1], sems), cost=4.0, aliases={4: 0}, name="depth",
    )(base, courant, *got_y, field)
    lifted, *sends = call(
        lift_x_kernel, whole(3), whole(3), [tall_shape, y_lift_shape, y_lift_shape],
        name="lift_x",
    )(lifted, got, got_2)
    got, got_2 = swap_y(sends[0]), swap_y_2(sends[1])
    halves = call(
        lift_y_local_kernel, whole(1), whole(2), [half_shape, half_shape], cost=4.0,
        name="lift_y_local",
    )(lifted)
    (snapshot_code,) = call(
        lift_y_kernel, whole(4), far(1), [natural],
        (pltpu.VMEM(block_shape, f32), pltpu.SemaphoreType.DMA((4, tiles))), name="lift_y",
    )(*halves, got, got_2)
    return (pressure_next, pressure_mid, snapshot_code)


def solution(mesh):
    block = P(("shot", "gx"), "gy", None)
    return jax.shard_map(
        shards,
        mesh=mesh,
        in_specs=(block, block, block, P(), P("shot"), P("shot"), P("shot")),
        out_specs=(block, block, block),
        check_vma=False,
    )
```

```python
import functools

import jax
import jax.numpy as jnp
from jax import lax
from jax.experimental import pallas as pl
from jax.experimental.pallas import tpu as pltpu
from jax.sharding import PartitionSpec as P


STENCIL_WEIGHTS = (-205.0 / 72.0, 8.0 / 5.0, -1.0 / 5.0, 8.0 / 315.0, -1.0 / 560.0)
LIFT_ALPHA = -1.586134342
LIFT_BETA = -0.05298011854
LIFT_GAMMA = 0.8829110762
LIFT_DELTA = 0.4435068522
LIFT_SCALE = 1.149604398
DEAD_ZONE = 0.25
QUANT_STEP = 0.5

HALO = 4
LANES = 128
SUB = 8


def iota(axis):
    return lax.broadcasted_iota(jnp.int32, (SUB, LANES), axis)


def rolled(value, shift, axis):
    size = value.shape[axis]
    shift = shift % size
    return value if shift == 0 else pltpu.roll(value, shift, axis)


def parity(axis):
    index = lax.axis_index(axis)
    return lax.rem(index, 2) == 0, index == 0, index == lax.axis_size(axis) - 1


def pack_x(field, low, high, even, x_first, x_second):
    for slot, (down, up) in enumerate(zip(low, high)):
        for tile in range(x_first.shape[1]):
            for y_tile in range(x_first.shape[2] // SUB):
                below, above = field(down, tile, y_tile), field(up, tile, y_tile)
                where = (slot, tile, pl.ds(y_tile * SUB, SUB))
                x_first[where] = jnp.where(even, above, below)
                x_second[where] = jnp.where(even, below, above)


def pack_y(rows, rows_x, tiles, even, y_first, y_second):
    def step(x, _):
        for tile in range(tiles):
            below, above = rows(x, tile)
            where = (x, tile // 2, pl.ds(tile % 2 * HALO, HALO))
            y_first[where] = jnp.where(even, above, below)
            y_second[where] = jnp.where(even, below, above)
        return 0

    lax.fori_loop(0, rows_x, step, 0, unroll=4)


def zero_pads(padded, rows_x, rows_y):
    zero = jnp.zeros((SUB, LANES), jnp.float32)
    tiles = padded.shape[1]
    for x in list(range(HALO)) + list(range(rows_x + HALO, rows_x + 2 * HALO)):
        for tile in range(tiles):
            for y in range(SUB, rows_y + SUB, SUB):
                padded[x, tile, pl.ds(y, SUB)] = zero

    def step(x, _):
        for tile in range(tiles):
            padded[x + HALO, tile, pl.ds(0, SUB)] = zero
            padded[x + HALO, tile, pl.ds(rows_y + SUB, SUB)] = zero
        return 0

    lax.fori_loop(0, rows_x, step, 0)


def padded_vector(padded):
    return lambda x, tile, y_tile: padded[x + HALO, tile, pl.ds(SUB + y_tile * SUB, SUB)]


def sends_kernel(now, x_first, x_second, y_first, y_second):
    rows_x, rows_y, depth = now.shape
    even_x, _, _ = parity("gx")
    even_y, _, _ = parity("gy")

    def field(x, tile, y_tile):
        return now[x, pl.ds(y_tile * SUB, SUB), pl.ds(tile * LANES, LANES)]

    pack_x(field, range(HALO), range(rows_x - HALO, rows_x), even_x, x_first, x_second)

    def rows(x, tile):
        z = pl.ds(tile * LANES, LANES)
        return now[x, pl.ds(0, HALO), z], now[x, pl.ds(rows_y - HALO, HALO), z]

    pack_y(rows, rows_x, depth // LANES, even_y, y_first, y_second)


def local_laplace(padded, x, tiles, y_tile):
    lane = iota(1)
    row, y = x + HALO, SUB + y_tile * SUB
    center = [padded[row, tile, pl.ds(y, SUB)] for tile in range(tiles)]
    zero = jnp.zeros((SUB, LANES), jnp.float32)
    total = [3.0 * STENCIL_WEIGHTS[0] * value for value in center]
    for offset in range(1, HALO + 1):
        up = [rolled(value, -offset, 1) for value in center] + [zero]
        down = [zero] + [rolled(value, offset, 1) for value in center]
        for tile in range(tiles):
            beside = jnp.where(lane < LANES - offset, up[tile], up[tile + 1])
            beside = beside + jnp.where(lane >= offset, down[tile + 1], down[tile])
            beside = beside + (
                padded[row + offset, tile, pl.ds(y, SUB)]
                + padded[row - offset, tile, pl.ds(y, SUB)]
            )
            beside = beside + (
                padded[row, tile, pl.ds(y + offset, SUB)]
                + padded[row, tile, pl.ds(y - offset, SUB)]
            )
            total[tile] = total[tile] + STENCIL_WEIGHTS[offset] * beside
    return center, total


def add_sources(base, cells, samples, wavelet, step_index, rows_x, rows_y, depth):
    all_y = rows_y * lax.axis_size("gy")
    start_x = lax.axis_index("gx") * rows_x
    start_y = lax.axis_index("gy") * rows_y
    lane = lax.broadcasted_iota(jnp.int32, (1, LANES), 1)
    for shot in range(cells.shape[0]):
        cell = cells[shot]
        x = lax.div(cell, all_y * depth) - start_x
        y = lax.rem(lax.div(cell, depth), all_y) - start_y
        z = lax.rem(cell, depth)
        inside = (x >= 0) & (x < rows_x) & (y >= 0) & (y < rows_y)

        @pl.when(inside)
        def _():
            value = wavelet[lax.rem(samples[shot] + step_index, wavelet.shape[0])]
            where = (x, lax.div(z, LANES), pl.ds(y, 1))
            base[where] = base[where] + jnp.where(lane == lax.rem(z, LANES), value, 0.0)


def start_all(copies):
    for copy in copies:
        copy.start()
    return copies


def wait_all(copies):
    for copy in copies:
        copy.wait()


def paired(sources, targets, sems):
    return [
        pltpu.make_async_copy(source, target, sems.at[place])
        for place, (source, target) in enumerate(zip(sources, targets))
    ]


def first_local_kernel(
    now, old, classes, table, wavelet, cells, samples,
    padded, base, courant, blank,
    old_here, classes_here, table_here, wavelet_here, cells_here, samples_here, sems,
):
    rows_x, rows_y, depth = old.shape
    tiles = depth // LANES
    lane = iota(1)
    copies = start_all(
        paired(
            (table, classes, old, wavelet, cells, samples),
            (table_here, classes_here, old_here, wavelet_here, cells_here, samples_here),
            sems,
        )
    )
    zero_pads(padded, rows_x, rows_y)

    def spread(x, _):
        for tile in range(tiles):
            for y in range(0, rows_y, SUB):
                padded[x + HALO, tile, pl.ds(SUB + y, SUB)] = now[
                    x, pl.ds(y, SUB), pl.ds(tile * LANES, LANES)
                ]
        return 0

    lax.fori_loop(0, rows_x, spread, 0, unroll=4)

    def sums(x, _):
        for y_tile in range(rows_y // SUB):
            _, total = local_laplace(padded, x, tiles, y_tile)
            for tile in range(tiles):
                base[x, tile, pl.ds(y_tile * SUB, SUB)] = total[tile]
        return 0

    lax.fori_loop(0, rows_x, sums, 0, unroll=4)
    wait_all(copies)
    entries = jnp.zeros((SUB, LANES), jnp.float32)
    for material in range(table.shape[0]):
        entries = jnp.where(lane == material, table_here[material], entries)

    def step(x, _):
        for y_tile in range(rows_y // SUB):
            y = pl.ds(y_tile * SUB, SUB)
            for tile in range(tiles):
                z = pl.ds(tile * LANES, LANES)
                speed = jnp.take_along_axis(entries, classes_here[x, y, z], axis=1)
                courant[x, tile, y] = speed
                base[x, tile, y] = (
                    2.0 * now[x, y, z] - old_here[x, y, z] + speed * base[x, tile, y]
                )
        return 0

    lax.fori_loop(0, rows_x, step, 0, unroll=4)
    add_sources(
        base, cells_here, samples_here, wavelet_here, 0, rows_x, rows_y, depth
    )
    zero_pads(blank, rows_x, rows_y)


def second_local_kernel(
    padded, before, courant, wavelet, cells, samples,
    base, mid,
    wavelet_here, cells_here, samples_here, sems,
):
    rows_x, rows_y, depth = mid.shape
    tiles = depth // LANES
    copies = start_all(
        paired(
            [wavelet, cells, samples]
            + [padded.at[pl.ds(HALO, rows_x), t, pl.ds(SUB, rows_y), :] for t in range(tiles)],
            [wavelet_here, cells_here, samples_here]
            + [mid.at[:, :, pl.ds(t * LANES, LANES)] for t in range(tiles)],
            sems,
        )
    )

    def step(x, _):
        for y_tile in range(rows_y // SUB):
            center, total = local_laplace(padded, x, tiles, y_tile)
            y = pl.ds(y_tile * SUB, SUB)
            for tile in range(tiles):
                earlier = before[x + HALO, tile, pl.ds(SUB + y_tile * SUB, SUB)]
                base[x, tile, y] = (
                    2.0 * center[tile] - earlier + courant[x, tile, y] * total[tile]
                )
        return 0

    lax.fori_loop(0, rows_x, step, 0, unroll=4)
    wait_all(copies)
    add_sources(
        base, cells_here, samples_here, wavelet_here, 1, rows_x, rows_y, depth
    )


def sides(first, second, even, at_end):
    second = jnp.where(at_end, 0.0, second)
    return jnp.where(even, second, first), jnp.where(even, first, second)


def add_halos(base, courant, x_first, x_second, y_first, y_second, x_halo, y_halo, rows, store):
    rows_x, tiles, rows_y, _ = base.shape
    y_tiles = rows_y // SUB
    even_x, first_x, last_x = parity("gx")
    even_y, first_y, last_y = parity("gy")
    end_x, end_y = first_x | last_x, first_y | last_y
    first_at = jnp.where(even_x, HALO, 0)
    zero = jnp.zeros((SUB, LANES), jnp.float32)
    for slot in range(HALO if x_halo is not None else 0):
        for tile in range(tiles):
            for y_tile in range(y_tiles):
                y = pl.ds(y_tile * SUB, SUB)
                x_halo[first_at + slot, tile, y] = x_first[slot, tile, y]
                second = x_second[slot, tile, y]
                x_halo[HALO - first_at + slot, tile, y] = jnp.where(end_x, 0.0, second)

    def spread(x):
        for tile in range(tiles):
            where = (x, tile // 2, pl.ds(tile % 2 * HALO, HALO))
            low, high = sides(y_first[where], y_second[where], even_y, end_y)
            y_halo[x, tile, pl.ds(HALO, SUB)] = zero
            y_halo[x, tile, pl.ds(SUB, SUB)] = zero
            y_halo[x, tile, pl.ds(0, HALO)] = low
            y_halo[x, tile, pl.ds(2 * SUB, HALO)] = high

    def finish(x, x_terms):
        for y_tile in range(y_tiles):
            y = pl.ds(y_tile * SUB, SUB)
            done = []
            for tile in range(tiles):
                beyond = None
                terms = [(w, x_halo[slot, tile, y]) for w, slot in x_terms]
                for offset in range(1, HALO + 1):
                    weight = STENCIL_WEIGHTS[offset]
                    if y_tile == 0:
                        terms.append((weight, y_halo[x, tile, pl.ds(HALO - offset, SUB)]))
                    if y_tile == y_tiles - 1:
                        terms.append((weight, y_halo[x, tile, pl.ds(SUB + offset, SUB)]))
                for weight, value in terms:
                    beyond = weight * value if beyond is None else beyond + weight * value
                value = base[x, tile, y]
                if beyond is not None:
                    value = value + courant[x, tile, y] * beyond
                done.append(value)
            store(x, y_tile, done)

    for x in rows:
        spread(x)
    for x in rows:
        x_terms = []
        for offset in range(1, HALO + 1):
            if x - offset < 0:
                x_terms.append((STENCIL_WEIGHTS[offset], HALO + x - offset))
            if x + offset >= rows_x:
                x_terms.append((STENCIL_WEIGHTS[offset], HALO + x + offset - rows_x))
        finish(x, x_terms)


def inner_rows(rows_x):
    return range(HALO, rows_x - HALO)


def outer_rows(rows_x):
    return [*range(HALO), *range(rows_x - HALO, rows_x)]


def mid_kernel(
    base, courant, x_in, x_in_2, y_in, y_in_2, blank,
    padded, x_first, x_second, y_first, y_second, x_halo, y_halo,
):
    rows_x, tiles, rows_y, _ = base.shape
    even_x, _, _ = parity("gx")
    even_y, _, _ = parity("gy")

    def store(x, y_tile, values):
        for tile, value in enumerate(values):
            padded[x + HALO, tile, pl.ds(SUB + y_tile * SUB, SUB)] = value

    add_halos(
        base, courant, x_in, x_in_2, y_in, y_in_2, x_halo, y_halo, range(rows_x), store
    )
    field = padded_vector(padded)
    pack_x(field, range(HALO), range(rows_x - HALO, rows_x), even_x, x_first, x_second)

    def rows(x, tile):
        y = SUB + rows_y - HALO
        return padded[x + HALO, tile, pl.ds(SUB, HALO)], padded[x + HALO, tile, pl.ds(y, HALO)]

    pack_y(rows, rows_x, tiles, even_y, y_first, y_second)


def lift_depth(first, second):
    lane = iota(1)
    early = lax.rem(lane, 2) == 0
    tiles = range(len(first))
    even = [jnp.where(early, a, rolled(b, 1, 1)) for a, b in zip(first, second)]
    odd = [jnp.where(early, rolled(a, -1, 1), b) for a, b in zip(first, second)]
    for weight_odd, weight_even in ((LIFT_ALPHA, LIFT_BETA), (LIFT_GAMMA, LIFT_DELTA)):
        up = [rolled(value, -2, 1) for value in even]
        up.append(even[-1])
        above = [jnp.where(lane < LANES - 2, up[t], up[t + 1]) for t in tiles]
        odd = [odd[t] + weight_odd * (even[t] + above[t]) for t in tiles]
        down = [odd[0]] + [rolled(value, 2, 1) for value in odd]
        below = [jnp.where(lane >= 2, down[t + 1], down[t]) for t in tiles]
        even = [even[t] + weight_even * (odd[t] + below[t]) for t in tiles]
    return (
        [jnp.where(early, e, rolled(o, 1, 1)) for e, o in zip(even, odd)],
        [jnp.where(early, rolled(e, -1, 1), o) for e, o in zip(even, odd)],
    )


def next_kernel(
    base, courant, x_in, x_in_2, y_in, y_in_2,
    field, x_first, x_second, x_halo, y_halo,
):
    rows_x, tiles, rows_y, _ = base.shape
    even_x, _, _ = parity("gx")

    def store(x, y_tile, values):
        y = pl.ds(y_tile * SUB, SUB)
        for tile, value in enumerate(values):
            field[x, tile, y] = value

    add_halos(
        base, courant, x_in, x_in_2, y_in, y_in_2, x_halo, y_halo, outer_rows(rows_x), store
    )
    for y_tile in range(rows_y // SUB):
        y = pl.ds(y_tile * SUB, SUB)
        rows = []
        for tile in range(tiles):
            start = [field[x, tile, y] for x in range(3)]
            end = [field[x, tile, y] for x in range(rows_x - 4, rows_x)]
            low = (start[0], start[1] + LIFT_ALPHA * (start[0] + start[2]))
            high = (
                end[2] + LIFT_BETA * (end[1] + LIFT_ALPHA * (end[0] + end[2])),
                end[3] + LIFT_ALPHA * end[2],
            )
            rows.append(low + high)
        for slot in range(2):
            low, high = lift_depth(
                [row[slot] for row in rows], [row[2 + slot] for row in rows]
            )
            for tile in range(tiles):
                x_first[slot, tile, y] = jnp.where(even_x, high[tile], low[tile])
                x_second[slot, tile, y] = jnp.where(even_x, low[tile], high[tile])


def outward(field, out, sems):
    tiles = field.shape[1]
    return paired(
        [field.at[:, tile] for tile in range(tiles)],
        [out.at[:, :, pl.ds(tile * LANES, LANES)] for tile in range(tiles)],
        sems,
    )


def depth_kernel(base, courant, y_in, y_in_2, edges, field, lifted, out, y_halo, sems):
    rows_x, tiles, rows_y, _ = base.shape

    def store(x, y_tile, values):
        for tile, value in enumerate(values):
            field[x, tile, pl.ds(y_tile * SUB, SUB)] = value

    add_halos(
        base, courant, None, None, y_in, y_in_2, None, y_halo, inner_rows(rows_x), store
    )
    copies = start_all(outward(field, out, sems))

    def step(x, _):
        for y in range(0, rows_y, 2 * SUB):
            here = pl.ds(y, SUB), pl.ds(y + SUB, SUB)
            pair = lift_depth(
                *([field[x, tile, part] for tile in range(tiles)] for part in here)
            )
            for part, values in zip(here, pair):
                for tile, value in enumerate(values):
                    lifted[x, tile, part] = value
        return 0

    lax.fori_loop(0, rows_x, step, 0, unroll=4)
    wait_all(copies)


def lift_x_kernel(lifted, x_in, x_in_2, out, y_first, y_second):
    rows_x, tiles, rows_y, _ = lifted.shape
    y_tiles = rows_y // SUB
    half = rows_x // 2
    even_x, first_x, last_x = parity("gx")
    even_y, _, _ = parity("gy")

    for tile in range(tiles):
        for y_tile in range(y_tiles):
            y = pl.ds(y_tile * SUB, SUB)
            got = [
                (
                    jnp.where(even_x, x_in_2[slot, tile, y], x_in[slot, tile, y]),
                    jnp.where(even_x, x_in[slot, tile, y], x_in_2[slot, tile, y]),
                )
                for slot in range(2)
            ]
            even = [lifted[2 * i, tile, y] for i in range(half)]
            odd = [lifted[2 * i + 1, tile, y] for i in range(half)]
            beyond = jnp.where(last_x, even[-1], got[0][1])
            even.append(beyond)
            odd = [odd[i] + LIFT_ALPHA * (even[i] + even[i + 1]) for i in range(half)]
            before = got[1][0] + LIFT_ALPHA * even[0]
            odd = [jnp.where(first_x, odd[0], before)] + odd
            last = even.pop() + LIFT_BETA * (odd[-1] + got[1][1])
            even = [even[i] + LIFT_BETA * (odd[i] + odd[i + 1]) for i in range(half)]
            even.append(jnp.where(last_x, even[-1], last))
            start = got[0][0] + LIFT_BETA * odd[0]
            start = odd[0] + LIFT_GAMMA * (start + even[0])
            odd = [odd[i + 1] + LIFT_GAMMA * (even[i] + even[i + 1]) for i in range(half)]
            padded = [jnp.where(first_x, odd[0], start)] + odd
            even = [even[i] + LIFT_DELTA * (padded[i] + padded[i + 1]) for i in range(half)]
            here = pl.ds(SUB + y_tile * SUB, SUB)
            for i in range(half):
                out[2 * i, tile, here] = even[i]
                out[2 * i + 1, tile, here] = odd[i]

    head = lax.broadcasted_iota(jnp.int32, (2, LANES), 0) == 0

    def pack(x, _):
        for tile in range(tiles):

            def rows(y):
                return out[x, tile, pl.ds(SUB + y, 2)]

            low = rows(0)
            low = low + jnp.where(head, 0.0, LIFT_ALPHA * (rows(-1) + rows(1)))
            end = rows_y - 2
            high, below = rows(end), rows(end - 1)
            more = LIFT_BETA * (below + LIFT_ALPHA * (rows(end - 2) + high))
            high = high + jnp.where(head, more, LIFT_ALPHA * below)
            where = (x, tile // 4, pl.ds(tile % 4 * 2, 2))
            y_first[where] = jnp.where(even_y, high, low)
            y_second[where] = jnp.where(even_y, low, high)
        return 0

    lax.fori_loop(0, rows_x, pack, 0, unroll=8)


def y_scales():
    z_odd = lax.rem(iota(1), 2) == 1

    def scale(x_odd, y_odd):
        power = (1 if x_odd else -1) + (1 if y_odd else -1)
        return jnp.where(
            z_odd, LIFT_SCALE ** (power + 1) / QUANT_STEP, LIFT_SCALE ** (power - 1) / QUANT_STEP
        )

    return [[scale(x_odd, y_odd) for y_odd in (False, True)] for x_odd in (False, True)]


def lift_y_local_kernel(lifted, out):
    rows_x, tiles, _, _ = lifted.shape
    _, first_y, last_y = parity("gy")
    sub = iota(0)
    top = sub == SUB - 1
    bottom = sub == 0
    at_first = bottom & first_y
    at_last = top & last_y
    scales = y_scales()

    def row(x, x_odd):
        for tile in range(tiles):
            even = lifted[x, tile, pl.ds(SUB, SUB, stride=2)]
            odd = lifted[x, tile, pl.ds(SUB + 1, SUB, stride=2)]
            beyond = jnp.where(at_last, even, jnp.where(top, 0.0, rolled(even, -1, 0)))
            odd = odd + LIFT_ALPHA * (even + beyond)
            before = LIFT_ALPHA * even
            under = jnp.where(at_first, odd, jnp.where(bottom, before, rolled(odd, 1, 0)))
            last = LIFT_BETA * odd
            even = even + LIFT_BETA * (odd + under)
            beyond = jnp.where(at_last, even, jnp.where(top, last, rolled(even, -1, 0)))
            start = before + LIFT_GAMMA * (LIFT_BETA * before + even)
            odd = odd + LIFT_GAMMA * (even + beyond)
            under = jnp.where(at_first, odd, jnp.where(bottom, start, rolled(odd, 1, 0)))
            even = even + LIFT_DELTA * (odd + under)
            out[x, tile, pl.ds(0, SUB, stride=2)] = even * scales[x_odd][0]
            out[x, tile, pl.ds(1, SUB, stride=2)] = odd * scales[x_odd][1]

    def step(pair, _):
        row(2 * pair, 0)
        row(2 * pair + 1, 1)
        return 0

    lax.fori_loop(0, rows_x // 2, step, 0, unroll=2)


def lift_y_kernel(local, y_in, y_in_2, out, codes, low_rows, high_rows, sems):
    rows_x, tiles, rows_y, _ = local.shape
    even_y, first_y, last_y = parity("gy")
    sub = iota(0)
    edge = DEAD_ZONE / QUANT_STEP
    a, b, g, d = LIFT_ALPHA, LIFT_BETA, LIFT_GAMMA, LIFT_DELTA
    far_odd = a + g * (1.0 + 2.0 * b * a)
    added = (
        ({0: d * g}, {0: b + d * (1.0 + 3.0 * g * b), 1: g * b, 2: d * g * b}),
        (
            {4: d * g * b * a, 5: g * b * a, 6: b * a + d * (g * b * a + far_odd), 7: far_odd},
            {6: d * g * b, 7: g * b},
        ),
    )

    def at(places, keep, scale):
        total = jnp.zeros((SUB, LANES), jnp.float32)
        for place, weight in places.items():
            total = jnp.where(sub == place, weight, total)
        return jnp.where(keep, total * scale, 0.0)

    weights = [
        [
            [at(places, keep, jnp.where(lax.rem(sub, 2) == 1, odd, even)) for places in rows]
            for rows, keep in zip(added, (~first_y, ~last_y))
        ]
        for even, odd in y_scales()
    ]

    def row(x):
        for group in range(y_in.shape[1]):
            first, second = y_in[x, group], y_in_2[x, group]
            low_rows[x, group] = jnp.where(even_y, second, first)
            high_rows[x, group] = jnp.where(even_y, first, second)
        for tile in range(tiles):
            for side, (rows, y) in enumerate(((low_rows, 0), (high_rows, rows_y - SUB))):
                value = local[x, tile, pl.ds(y, SUB)]
                for slot in range(2):
                    place = pl.ds(tile % 4 * 2 + slot, 1)
                    beyond = jnp.broadcast_to(rows[x, tile // 4, place], (SUB, LANES))
                    value = value + weights[x % 2][side][slot] * beyond
                codes[x, pl.ds(y, SUB), pl.ds(tile * LANES, LANES)] = value - jnp.minimum(
                    jnp.maximum(value, -edge), edge
                )

    chunk = rows_x // 4
    copies = paired(
        [codes.at[pl.ds(part * chunk, chunk)] for part in range(4)],
        [out.at[pl.ds(part * chunk, chunk)] for part in range(4)],
        sems,
    )
    for part in range(4):
        for x in range(part * chunk, (part + 1) * chunk):
            row(x)
        copies[part].start()
    wait_all(copies)


def whole(count):
    return [pl.BlockSpec(memory_space=pltpu.VMEM)] * count


def far(count):
    return [pl.BlockSpec(memory_space=pltpu.HBM)] * count


def call(kernel, in_specs, out_specs, out_shape, scratch=(), cost=1.0, aliases=None, **kwargs):
    return pl.pallas_call(
        kernel,
        in_specs=in_specs,
        out_specs=out_specs,
        out_shape=[jax.ShapeDtypeStruct(shape, jnp.float32) for shape in out_shape],
        scratch_shapes=list(scratch),
        input_output_aliases=aliases or {},
        compiler_params=pltpu.CompilerParams(vmem_limit_bytes=16 << 20),
        cost_estimate=pl.CostEstimate(
            flops=int(cost * 1e6), bytes_accessed=int(cost * 1e6), transcendentals=0
        ),
        **kwargs,
    )


def swaps(names, counts, partner):
    pairs = []
    for y in range(counts[0]):
        for x in range(counts[1]):
            target = partner(y, x)
            pairs.append((y * counts[1] + x, target[0] * counts[1] + target[1]))
    return functools.partial(lax.ppermute, axis_name=names, perm=pairs)


def exchanges(count_y, count_x):
    names = ("gy", "gx")
    counts = (count_y, count_x)

    def second(index, count):
        return (index + 1) % count if index % 2 else (index - 1) % count

    x_first = swaps(names, counts, lambda y, x: (y, x ^ 1))
    x_second = swaps(names, counts, lambda y, x: (y, second(x, count_x)))
    y_first = swaps(names, counts, lambda y, x: (y ^ 1, x))

    def inner_y(y, x):
        return (second(y, count_y), x) if 0 < y < count_y - 1 else (y, x ^ 1)

    return x_first, x_second, y_first, swaps(names, counts, inner_y)


def shards(pressure_now, pressure_old, classes, class_table, wavelet, source_cells, samples):
    rows_x, rows_y, depth = pressure_now.shape
    tiles = depth // LANES
    assert rows_y == 2 * SUB and tiles % 4 == 0
    swap_x, swap_x_2, swap_y, swap_y_2 = exchanges(lax.axis_size("gy"), lax.axis_size("gx"))
    padded_shape = (rows_x + 2 * HALO, tiles, rows_y + 2 * SUB, LANES)
    block_shape = (rows_x, tiles, rows_y, LANES)
    x_shape = (HALO, tiles, rows_y, LANES)
    y_shape = (rows_x, tiles // 2, SUB, LANES)
    x_lift_shape = (2, tiles, rows_y, LANES)
    y_lift_shape = (rows_x, tiles // 4, SUB, LANES)
    tall_shape = (rows_x, tiles, rows_y + 2 * SUB, LANES)
    natural = (rows_x, rows_y, depth)
    sems = pltpu.SemaphoreType.DMA((tiles,))
    halos = (
        pltpu.VMEM((2 * HALO, tiles, rows_y, LANES), jnp.float32),
        pltpu.VMEM((rows_x, tiles, 3 * SUB, LANES), jnp.float32),
    )

    def star(sends):
        got = []
        for place, swap in enumerate((swap_x, swap_x_2, swap_y, swap_y_2)):
            got.append(swap(sends[place]))
        return got

    f32 = jnp.float32
    scalar_memory = (
        pltpu.SMEM(wavelet.shape, f32),
        pltpu.SMEM(source_cells.shape, jnp.int32),
        pltpu.SMEM(samples.shape, jnp.int32),
    )
    pressure_old, classes, class_table, wavelet, source_cells, samples = (
        pltpu.with_memory_space_constraint(array, pltpu.HBM)
        for array in (pressure_old, classes, class_table, wavelet, source_cells, samples)
    )
    sends = call(
        sends_kernel, whole(1), whole(4), [x_shape, x_shape, y_shape, y_shape], name="sends"
    )(pressure_now)
    got = star(sends)
    now, base, courant, blank = call(
        first_local_kernel, whole(1) + far(6), whole(4),
        [padded_shape, block_shape, block_shape, padded_shape],
        (
            pltpu.VMEM(natural, f32), pltpu.VMEM(natural, jnp.int32),
            pltpu.SMEM(class_table.shape, f32), *scalar_memory,
            pltpu.SemaphoreType.DMA((6,)),
        ),
        cost=4.0, name="first_local",
    )(pressure_now, pressure_old, classes, class_table, wavelet, source_cells, samples)
    mid, *sends = call(
        mid_kernel, whole(7), whole(5), [padded_shape, x_shape, x_shape, y_shape, y_shape],
        halos, aliases={6: 0}, name="mid",
    )(base, courant, *got, blank)
    got = star(sends)
    base, pressure_mid = call(
        second_local_kernel, whole(3) + far(3), whole(1) + far(1), [block_shape, natural],
        (*scalar_memory, pltpu.SemaphoreType.DMA((tiles + 3,))), cost=4.0, name="second_local",
    )(mid, now, courant, wavelet, source_cells, samples)
    field, *sends = call(
        next_kernel, whole(6), whole(3), [block_shape, x_lift_shape, x_lift_shape],
        halos, name="next",
    )(base, courant, *got)
    got_y = got[2:]
    got_2, got = swap_x_2(sends[1]), swap_x(sends[0])
    _, lifted, pressure_next = call(
        depth_kernel, whole(5), whole(2) + far(1), [block_shape, block_shape, natural],
        (halos[1], sems), cost=4.0, aliases={4: 0}, name="depth",
    )(base, courant, *got_y, field)
    lifted, *sends = call(
        lift_x_kernel, whole(3), whole(3), [tall_shape, y_lift_shape, y_lift_shape],
        name="lift_x",
    )(lifted, got, got_2)
    got, got_2 = swap_y(sends[0]), swap_y_2(sends[1])
    (local,) = call(
        lift_y_local_kernel, whole(1), whole(1), [block_shape], cost=4.0, name="lift_y_local"
    )(lifted)
    (snapshot_code,) = call(
        lift_y_kernel, whole(3), far(1), [natural],
        (
            pltpu.VMEM(natural, f32), pltpu.VMEM(y_lift_shape, f32), pltpu.VMEM(y_lift_shape, f32),
            pltpu.SemaphoreType.DMA((4,)),
        ),
        name="lift_y",
    )(local, got, got_2)
    return (pressure_next, pressure_mid, snapshot_code)


def solution(mesh):
    block = P(("shot", "gx"), "gy", None)
    return jax.shard_map(
        shards,
        mesh=mesh,
        in_specs=(block, block, block, P(), P("shot"), P("shot"), P("shot")),
        out_specs=(block, block, block),
        check_vma=False,
    )
```
